1024 devices in a mesh: seq: 8 (over x, core), chan: 128 (over y, z).
Axes of the slice: x: 4, y: 4, z: 32, core: 2. Of those that a mesh axis runs over, the one named last changes fastest.
Arguments:
- projections: bfloat16 [3, 2048, 16384], P(None, 'chan', 'seq'), may hold values from -6 to 6
- filter_taps: float32 [2048, 16384], P('chan', 'seq'), may hold values from -1.3 to 1.3
- skip_gain: float32 [2048], P('chan'), may hold values from -1 to 1
- head_weight: bfloat16 [2048, 3840], P('chan'), may hold values from -0.75 to 0.75
- head_bias: float32 [3840], replicated, may hold values from -1 to 1
- counts: int32 [512, 3840], P('seq'), may hold values from 0 to 11
Outputs:
- mean_loss: float32 [], replicated
- feature_grads: float32 [3, 2048, 16384], P(None, 'chan', 'seq')
The draws below stay inside these ranges and needn't reach their ends.
All inputs are finite; a program needn't handle non-finite values.
Results may differ from the reference program's by a relative error of at most 0.007.
Values may be sent and summed in bfloat16 or wider, within the bound.
A program may use at most 32 MiB of HBM per device.

```python
import jax
import jax.numpy as jnp
from jax import lax

CH = 2048
TRACKS = 3840
POOL = 32
SEQ = 16384
BINS = 512


def draw_filter_taps(key, part):
    key_tau, key_noise = jax.random.split(key)
    low = jnp.log(jnp.float32(30.0))
    noise = jnp.clip(jax.random.normal(key_noise, (CH, SEQ), jnp.float32), -5.0, 5.0)
    high = jnp.log(jnp.float32(64.0 * SEQ))
    tau = jnp.exp(jax.random.uniform(key_tau, (CH, 1), jnp.float32, 0.0, 1.0) * (high - low) + low)
    steps = jnp.arange(SEQ, dtype=jnp.float32)[None, :]
    envelope = jnp.exp(-steps / tau)
    scale = jnp.sqrt((1.0 - jnp.exp(-2.0 / tau)) / (1.0 - jnp.exp(-2.0 * SEQ / tau)))
    return (noise * envelope * scale).astype(jnp.float32)


def draw_counts(key, part):
    bins = jnp.arange(BINS, dtype=jnp.int32)
    upper = 4 + 9 * bins // BINS
    upper = jnp.broadcast_to(upper[:, None], (BINS, TRACKS))
    return jax.random.randint(key, (BINS, TRACKS), 0, upper, dtype=jnp.int32)


def levels(own_key, dims, shards, least, largest):
    level, own = 1.0, jax.random.fold_in(own_key, 6)
    for position, parts in shards:
        heights = jnp.exp(jax.random.uniform(jax.random.fold_in(own, position), (parts,), jnp.float32, least / len(shards), largest / len(shards)))
        level = level * jnp.repeat(heights, dims[position] // parts).reshape([-1 if axis == position else 1 for axis in range(len(dims))])
    return level


def normal_values(stream_key, shape, deviation, most, cuts=(), held_as=jnp.bfloat16):
    factor_of = levels(stream_key, shape, cuts, -0.22, 0.18) if cuts else 1.0
    result = jax.random.normal(stream_key, shape, jnp.float32) * deviation * factor_of
    return jnp.minimum(jnp.maximum(result, -most), most).astype(held_as)


def setup_inputs(seed: int = 0) -> dict:
    key_list = jax.random.split(jax.random.key(seed), 7)
    projections = normal_values(key_list[0], (3, CH, SEQ), 1.0, 6.0, ((1, 128), (2, 8)))
    filter_taps = draw_filter_taps(jax.random.fold_in(key_list[6], 71), 0)
    skip_gain = jnp.clip(jax.random.uniform(key_list[2], (CH,), jnp.float32, -1.0, 1.0) * levels(key_list[2], (CH,), ((0, 128),), -0.4, 0.0), -1.0, 1.0)
    head_weight = normal_values(key_list[3], (CH, TRACKS), (CH // POOL) ** -0.5, 0.75, ((0, 128),))
    head_bias = jnp.clip(jax.random.uniform(key_list[4], (TRACKS,), jnp.float32, -1.0, 1.0), -1.0, 1.0)
    counts = draw_counts(jax.random.fold_in(key_list[6], 71), 0)
    return dict(projections=projections, filter_taps=filter_taps, skip_gain=skip_gain, head_weight=head_weight, head_bias=head_bias, counts=counts)


total_weight = 0.2
rate_floor = 0.5


def causal_block(pair):
    signal, taps = pair
    length = signal.shape[-1]
    padded_len = 2 * length
    spectrum = jnp.fft.rfft(signal, padded_len, axis=-1) * jnp.fft.rfft(taps, padded_len, axis=-1)
    return jnp.fft.irfft(spectrum, padded_len, axis=-1)[..., :length]


def anti_block(pair):
    signal, taps = pair
    length = signal.shape[-1]
    padded_len = 2 * length
    spectrum = jnp.fft.rfft(signal, padded_len, axis=-1) * jnp.conj(jnp.fft.rfft(taps, padded_len, axis=-1))
    return jnp.fft.irfft(spectrum, padded_len, axis=-1)[..., :length]


def blockwise(block_fn, signal, taps):
    groups = 16
    shaped = (signal.reshape(groups, -1, signal.shape[-1]), taps.reshape(groups, -1, taps.shape[-1]))
    return lax.map(block_fn, shaped).reshape(signal.shape)


def reference(projections, filter_taps, skip_gain, head_weight, head_bias, counts):
    query = projections[0].astype(jnp.float32)
    keyed = projections[1].astype(jnp.float32)
    valued = projections[2].astype(jnp.float32)
    key_value = keyed * valued
    conv = blockwise(causal_block, key_value, filter_taps)
    mixed = conv + skip_gain[:, None] * key_value
    output = query * mixed
    pooled = output.reshape(CH, BINS, POOL).mean(axis=2).astype(jnp.bfloat16)
    logits = jnp.dot(pooled.T, head_weight, preferred_element_type=jnp.float32) + head_bias[None, :]
    rates = jax.nn.softplus(logits) + rate_floor
    observed = counts.astype(jnp.float32)
    pred_total = jnp.sum(rates, axis=0)
    obs_total = jnp.sum(observed, axis=0)
    log_pred = jnp.log(pred_total)
    log_sum = jnp.sum(observed * jnp.log(rates))
    loss_sum = jnp.sum(total_weight * (pred_total - obs_total * log_pred) + obs_total * log_pred) - log_sum
    mean_loss = loss_sum / (BINS * TRACKS)
    ratio = obs_total / pred_total
    grad_rates = total_weight * (1.0 - ratio)[None, :] + ratio[None, :] - observed / rates
    grad_logits = (grad_rates * jax.nn.sigmoid(logits)).astype(jnp.bfloat16)
    grad_pooled = jnp.dot(head_weight, grad_logits.T, preferred_element_type=jnp.float32)
    grad_output = jnp.broadcast_to(grad_pooled[:, :, None] / POOL, (CH, BINS, POOL)).reshape(CH, SEQ)
    grad_query = grad_output * mixed
    gated = grad_output * query
    grad_kv = blockwise(anti_block, gated, filter_taps) + skip_gain[:, None] * gated
    return mean_loss, jnp.stack([grad_query, grad_kv * valued, grad_kv * keyed], axis=0)
```

```python
import math

import jax
import jax.numpy as jnp
from jax import lax
from jax.experimental import pallas as pl
from jax.experimental.pallas import tpu as pltpu
from jax.sharding import PartitionSpec as P

POOL = 32
NY = 4
NZ = 32
NS = 8
TR = 120
MESH = pl.DeviceIdType.MESH

total_weight = 0.2
rate_floor = 0.5


def head_kernel(
    w_ref, p_ref, cnt_ref, bias_ref,
    gp_ref, loss_ref,
    wa, wg, py, pg, ty, ts, gg,
    s_loc, s_wa, r_wa, s_wb, r_wb, s_wy, r_wy, s_py, r_py, s_pf, r_pf, s_pn, r_pn,
    s_ty, r_ty, s_ts, r_ts, s_gf, r_gf, s_gn, r_gn, s_gy, r_gy,
):
    s = lax.axis_index("seq")
    ch = lax.axis_index("chan")
    y = ch // NZ
    z = ch % NZ

    def zdev(d):
        return (s, y * NZ + (z + d + NZ) % NZ)

    def ydev(d):
        return (s, ((y + d) % NY) * NZ + z)

    def sdev(d):
        return ((s + d) % NS, ch)

    def send(src, dst, ss, rs, dev):
        c = pltpu.make_async_remote_copy(
            src_ref=src, dst_ref=dst, send_sem=ss, recv_sem=rs, device_id=dev, device_id_type=MESH
        )
        c.start()
        return c

    near = ((0, -1), (2, 1), (3, 2))

    barrier = pltpu.get_barrier_semaphore()
    peers = [sdev(d) for d in range(1, NS)] + [ydev(d) for d in range(1, NY)]
    peers += [zdev(4 * k) for k in range(1, 8)] + [zdev(d) for d in (-2, -1, 1, 2)]
    for dev in peers:
        pl.semaphore_signal(barrier, inc=1, device_id=dev, device_id_type=MESH)
    pl.semaphore_wait(barrier, len(peers))

    c_wa = [send(w_ref.at[:, m], wa.at[m], s_wa.at[m], r_wa.at[m], zdev(o)) for m, o in near]
    c_py = [
        send(p_ref.at[d], py.at[d - 1], s_py.at[d], r_py.at[d], ydev(d)) for d in range(1, NY)
    ]
    own = pltpu.make_async_copy(w_ref.at[:, 1], wa.at[1], s_loc.at[0])
    own.start()
    own.wait()
    for c in c_wa:
        c.wait_recv()
    c_wb = [
        send(wa.at[:, k], wg.at[0, k], s_wb.at[k], r_wb.at[k], zdev(4 * k)) for k in range(1, 8)
    ]
    own = pltpu.make_async_copy(wa.at[:, 0], wg.at[0, 0], s_loc.at[1])
    own.start()

    for c in c_py:
        c.wait_recv()
    tile = p_ref[0].astype(jnp.float32)
    for d in range(NY - 1):
        tile = tile + py[d].astype(jnp.float32)
    pg[1, 0] = tile.astype(jnp.bfloat16)
    c_pf = [
        send(pg.at[1, 0], pg.at[1, k], s_pf.at[k], r_pf.at[k], zdev(4 * k)) for k in range(1, 8)
    ]
    for c in c_pf:
        c.wait_recv()
    c_pn = [send(pg.at[1], pg.at[m], s_pn.at[m], r_pn.at[m], zdev(o)) for m, o in near]

    own.wait()
    for c in c_wb:
        c.wait_recv()
    c_wy = [
        send(wg.at[0], wg.at[d], s_wy.at[d], r_wy.at[d], ydev(d)) for d in range(1, NY)
    ]
    for c in c_pn:
        c.wait_recv()
    for c in c_wy:
        c.wait_recv()

    logits = jnp.broadcast_to(bias_ref[0:1, :], (16, 128))
    for k in range(8):
        for m in range(4):
            rows = jnp.concatenate([wg[d, k, m] for d in range(NY)], axis=0)
            logits = logits + lax.dot_general(
                pg[m, k][:, :64], rows, (((1,), (0,)), ((), ())),
                preferred_element_type=jnp.float32,
            )
    rates = jnp.maximum(logits, 0.0) + jnp.log1p(jnp.exp(-jnp.abs(logits))) + rate_floor
    observed = cnt_ref[...].astype(jnp.float32)
    part = [
        jnp.sum(rates, axis=0, keepdims=True),
        jnp.sum(observed, axis=0, keepdims=True),
        jnp.sum(observed * jnp.log(rates), axis=0, keepdims=True),
        jnp.zeros((5, 128), jnp.float32),
    ]
    ty[0] = jnp.concatenate(part, axis=0)
    c_ty = [send(ty.at[0], ty.at[d], s_ty.at[d], r_ty.at[d], ydev(d)) for d in range(1, NY)]
    sig = 1.0 / (1.0 + jnp.exp(-logits))
    obs_rate = observed / rates
    for c in c_ty:
        c.wait_recv()
    tot = ty[y]
    for a in range(1, NY):
        tot = tot + ty[(y + NY - a) % NY]
    ts[0] = tot
    c_ts = [send(ts.at[0], ts.at[d], s_ts.at[d], r_ts.at[d], sdev(d)) for d in range(1, NS)]
    for c in c_ts:
        c.wait_recv()
    tot = ts[s]
    for a in range(1, NS):
        tot = tot + ts[(s + NS - a) % NS]
    pred = tot[0:1, :]
    obs = tot[1:2, :]
    log_pred = jnp.log(pred)
    lane = lax.broadcasted_iota(jnp.int32, (1, 128), 1)
    terms = total_weight * (pred - obs * log_pred) + obs * log_pred - tot[2:3, :]
    loss = jnp.sum(jnp.where(lane < TR, terms, 0.0), axis=1, keepdims=True)
    ratio = obs / pred
    grad_rates = total_weight * (1.0 - ratio) + ratio - obs_rate
    grad = grad_rates * sig
    hi = loss.astype(jnp.bfloat16).astype(jnp.float32)
    mid = (loss - hi).astype(jnp.bfloat16).astype(jnp.float32)
    lo = loss - hi - mid
    lanes = lax.broadcasted_iota(jnp.int32, (16, 128), 1)
    grad = jnp.where(
        lanes < TR, grad, jnp.where(lanes == TR, hi, jnp.where(lanes == TR + 1, mid, lo))
    )
    gg[0, 1, 0] = grad.astype(jnp.bfloat16)
    c_gf = [
        send(gg.at[0, 1, 0], gg.at[0, 1, k], s_gf.at[k], r_gf.at[k], zdev(-4 * k))
        for k in range(1, 8)
    ]
    for c in c_gf:
        c.wait_recv()
    c_gn = [
        send(gg.at[0, 1], gg.at[0, m], s_gn.at[m], r_gn.at[m], zdev(-o)) for m, o in near
    ]
    c_gy = [
        send(gg.at[0, 1], gg.at[d, 1], s_gy.at[d, 1], r_gy.at[d, 1], ydev(d))
        for d in range(1, NY)
    ]
    for c, (m, o) in zip(c_gn, near):
        c.wait_recv()
        c_gy += [
            send(gg.at[0, m], gg.at[d, m], s_gy.at[d, m], r_gy.at[d, m], ydev(d))
            for d in range(1, NY)
        ]

    by_z = jnp.zeros((1, 128), jnp.float32)
    for k in range(8):
        for m in range(4):
            row = gg[0, m, k][0:1, :].astype(jnp.float32)
            val = jnp.sum(
                jnp.where((lane >= TR) & (lane < TR + 3), row, 0.0), axis=1, keepdims=True
            )
            by_z = jnp.where(lane == (z + m - 1 + 4 * k + NZ) % NZ, val, by_z)
    loss_ref[...] = jnp.broadcast_to(jnp.sum(by_z, axis=1, keepdims=True), (8, 128))

    wl = jnp.concatenate([w_ref[k, m] for k in range(8) for m in range(4)], axis=1)

    def grad_block(d):
        gl = jnp.concatenate([gg[d, m, k] for k in range(8) for m in range(4)], axis=1)
        return lax.dot_general(
            wl, gl, (((1,), (1,)), ((), ())), preferred_element_type=jnp.float32
        )

    gp_ref[0] = grad_block(0)
    for c in c_gy:
        c.wait_recv()
    for d in range(1, NY):
        gp_ref[d] = grad_block(d)

    for c in c_wa + c_py + c_wb + c_pf + c_pn + c_wy + c_ty + c_ts + c_gf + c_gn + c_gy:
        c.wait_send()


def head(pooled, head_weight, head_bias, counts):
    ch = lax.axis_index("chan")
    y = ch // NZ
    z = ch % NZ
    w = jnp.pad(head_weight.reshape(16, NZ, TR), ((0, 0), (0, 0), (0, 128 - TR)))
    w = jnp.transpose(w, (1, 0, 2))
    w = lax.dynamic_slice_in_dim(jnp.concatenate([w, w], axis=0), (z + NZ - 1) % NZ, NZ, 0)
    w = w.reshape(8, 4, 16, 128)
    pt = pooled.T
    pt = lax.dynamic_slice_in_dim(jnp.concatenate([pt, pt], axis=0), y * 16, 64, 0)
    pt = pt.reshape(NY, 16, 16)
    pt = jnp.stack([jnp.pad(pt[d], ((0, 0), (16 * d, 112 - 16 * d))) for d in range(NY)])
    cnt = lax.dynamic_slice(counts, (y * 16, z * TR), (16, TR))
    cnt = jnp.pad(cnt, ((0, 0), (0, 128 - TR)))
    bias = jnp.pad(lax.dynamic_slice_in_dim(head_bias, z * TR, TR, 0), (0, 128 - TR))
    bias = jnp.broadcast_to(bias[None, :], (8, 128))
    sem = pltpu.SemaphoreType.DMA
    b16 = jnp.bfloat16
    gp, loss = pl.pallas_call(
        head_kernel,
        out_shape=(
            jax.ShapeDtypeStruct((NY, 16, 16), jnp.float32),
            jax.ShapeDtypeStruct((8, 128), jnp.float32),
        ),
        in_specs=[pl.BlockSpec(memory_space=pltpu.VMEM)] * 4,
        out_specs=(pl.BlockSpec(memory_space=pltpu.VMEM),) * 2,
        scratch_shapes=[
            pltpu.VMEM((4, 8, 16, 128), b16),
            pltpu.VMEM((4, 8, 4, 16, 128), b16),
            pltpu.VMEM((3, 16, 128), b16),
            pltpu.VMEM((4, 8, 16, 128), b16),
            pltpu.VMEM((4, 8, 128), jnp.float32),
            pltpu.VMEM((8, 8, 128), jnp.float32),
            pltpu.VMEM((4, 4, 8, 16, 128), b16),
            sem((2,)),
            sem((4,)), sem((4,)), sem((8,)), sem((8,)), sem((4,)), sem((4,)),
            sem((4,)), sem((4,)), sem((8,)), sem((8,)), sem((4,)), sem((4,)),
            sem((4,)), sem((4,)), sem((8,)), sem((8,)), sem((8,)), sem((8,)),
            sem((4,)), sem((4,)), sem((4, 4)), sem((4, 4)),
        ],
        compiler_params=pltpu.CompilerParams(collective_id=0, has_side_effects=True),
    )(w, pt, cnt, bias)
    gp = jnp.transpose(gp, (1, 0, 2))[:, ::-1].reshape(16, 64)
    gp = lax.dynamic_slice_in_dim(
        jnp.concatenate([gp, gp], axis=1), (3 + NY - y) % NY * 16, 64, 1
    )
    return loss[0, 0], gp


def split_length(padded_len):
    best = 1
    factor = 1
    while factor * factor <= padded_len:
        if padded_len % factor == 0:
            best = factor
        factor = factor + 1
    return (padded_len // best, best)


def dft_tables(outer, inner, padded_len):
    outer_idx = jnp.arange(outer, dtype=jnp.int32)
    inner_idx = jnp.arange(inner, dtype=jnp.int32)
    outer_angle = (
        2.0
        * math.pi
        * (outer_idx[:, None] * outer_idx[None, :] % outer).astype(jnp.float32)
        / outer
    )
    inner_angle = (
        2.0
        * math.pi
        * (inner_idx[:, None] * inner_idx[None, :] % inner).astype(jnp.float32)
        / inner
    )
    twist_angle = (
        2.0
        * math.pi
        * (outer_idx[:, None] * inner_idx[None, :] % padded_len).astype(jnp.float32)
        / padded_len
    )
    return (
        jnp.cos(outer_angle),
        -jnp.sin(outer_angle),
        jnp.cos(inner_angle),
        -jnp.sin(inner_angle),
        jnp.cos(twist_angle),
        -jnp.sin(twist_angle),
    )


def forward(real_in, tables):
    outer_re, outer_im, inner_re, inner_im, twist_re, twist_im = tables
    highest = lax.Precision.HIGHEST
    first_re = jnp.einsum("ka,mab->mkb", outer_re, real_in, precision=highest)
    first_im = jnp.einsum("ka,mab->mkb", outer_im, real_in, precision=highest)
    turned_re = first_re * twist_re - first_im * twist_im
    turned_im = first_re * twist_im + first_im * twist_re
    spec_re = jnp.einsum("mkb,bj->mkj", turned_re, inner_re, precision=highest) - jnp.einsum(
        "mkb,bj->mkj", turned_im, inner_im, precision=highest
    )
    spec_im = jnp.einsum("mkb,bj->mkj", turned_re, inner_im, precision=highest) + jnp.einsum(
        "mkb,bj->mkj", turned_im, inner_re, precision=highest
    )
    return (spec_re, spec_im)


def inverse(spec_re, spec_im, tables, padded_len):
    outer_re, outer_im, inner_re, inner_im, twist_re, twist_im = tables
    highest = lax.Precision.HIGHEST
    back_re = jnp.einsum("mkj,bj->mkb", spec_re, inner_re, precision=highest) + jnp.einsum(
        "mkj,bj->mkb", spec_im, inner_im, precision=highest
    )
    back_im = jnp.einsum("mkj,bj->mkb", spec_im, inner_re, precision=highest) - jnp.einsum(
        "mkj,bj->mkb", spec_re, inner_im, precision=highest
    )
    turned_re = back_re * twist_re + back_im * twist_im
    turned_im = back_im * twist_re - back_re * twist_im
    result = jnp.einsum("ka,mkb->mab", outer_re, turned_re, precision=highest) + jnp.einsum(
        "ka,mkb->mab", outer_im, turned_im, precision=highest
    )
    return result / padded_len


def to_pencil(stacked):
    return lax.all_to_all(stacked, "seq", split_axis=1, concat_axis=2, tiled=True)


def from_pencil(pencil_rows):
    return lax.all_to_all(pencil_rows, "seq", split_axis=1, concat_axis=0, tiled=True)


def pad_fold(pencil, outer, inner):
    padded = jnp.concatenate([pencil, jnp.zeros_like(pencil)], axis=2)
    return padded.reshape(-1, outer, inner)


def per_device(projections, filter_taps, skip_gain, head_weight, head_bias, counts):
    query = projections[0].astype(jnp.float32)
    keyed = projections[1].astype(jnp.float32)
    valued = projections[2].astype(jnp.float32)
    channels, width = keyed.shape
    bins = width // POOL
    seq_count = lax.axis_size("seq")
    tracks = head_weight.shape[1]
    key_value = keyed * valued
    pencil = to_pencil(jnp.stack([key_value, filter_taps], axis=0))
    pencil_ch = pencil.shape[1]
    length = pencil.shape[2]
    padded_len = 2 * length
    outer, inner = split_length(padded_len)
    tables = dft_tables(outer, inner, padded_len)
    spec_re, spec_im = forward(pad_fold(pencil, outer, inner), tables)
    signal_re = spec_re[:pencil_ch]
    signal_im = spec_im[:pencil_ch]
    taps_re = spec_re[pencil_ch:]
    taps_im = spec_im[pencil_ch:]
    prod_re = signal_re * taps_re - signal_im * taps_im
    prod_im = signal_re * taps_im + signal_im * taps_re
    conv_pencil = inverse(prod_re, prod_im, tables, padded_len).reshape(pencil_ch, padded_len)[
        :, :length
    ]
    conv = from_pencil(conv_pencil)
    mixed = conv + skip_gain[:, None] * key_value
    output = query * mixed
    pooled = output.reshape(channels, bins, POOL).mean(axis=2).astype(jnp.bfloat16)
    loss_sum, grad_pooled = head(pooled, head_weight, head_bias, counts)
    mean_loss = loss_sum / (bins * seq_count * tracks)
    grad_output = jnp.broadcast_to(grad_pooled[:, :, None] / POOL, (channels, bins, POOL)).reshape(
        channels, width
    )
    grad_query = grad_output * mixed
    gated = grad_output * query
    back_pencil = to_pencil(gated[None])
    back_re, back_im = forward(pad_fold(back_pencil, outer, inner), tables)
    corr_re = taps_re * back_re + taps_im * back_im
    corr_im = taps_re * back_im - taps_im * back_re
    corr_pencil = inverse(corr_re, corr_im, tables, padded_len).reshape(pencil_ch, padded_len)[
        :, :length
    ]
    grad_kv = from_pencil(corr_pencil) + skip_gain[:, None] * gated
    return (mean_loss, jnp.stack([grad_query, grad_kv * valued, grad_kv * keyed], axis=0))


def solution(mesh):
    placed = (
        P(None, "chan", "seq"),
        P("chan", "seq"),
        P("chan"),
        P("chan", None),
        P(),
        P("seq", None),
    )
    return jax.shard_map(
        per_device,
        mesh=mesh,
        in_specs=placed,
        out_specs=(P(), P(None, "chan", "seq")),
        check_vma=False,
    )
```

```python
import jax
import jax.numpy as jnp
from jax import lax
from jax.experimental import pallas as pl
from jax.experimental.pallas import tpu as pltpu
from jax.sharding import PartitionSpec as P

POOL = 32
NY = 4
NZ = 32
NS = 8
TR = 120
MESH = pl.DeviceIdType.MESH

total_weight = 0.2
rate_floor = 0.5


def step_kernel(
    x_ref, h_ref, skip_ref, w_ref, cnt_ref, bias_ref,
    out_ref, loss_ref,
    kv, hx, rx, xp, hf, sh, tt, yy, cv, oo, gx, gg_out, gr, pp,
    wa, wg, py, pg, ty, ts, gg,
    s_loc, s_kv, r_kv, s_hx, r_hx, s_cv, r_cv, s_gx, r_gx, s_gr, r_gr,
    s_wa, r_wa, s_wb, r_wb, s_wy, r_wy, s_py, r_py, s_pf, r_pf, s_pn, r_pn,
    s_ty, r_ty, s_ts, r_ts, s_gf, r_gf, s_gn, r_gn, s_gy, r_gy,
):
    s = lax.axis_index("seq")
    ch = lax.axis_index("chan")
    y = ch // NZ
    z = ch % NZ

    def zdev(d):
        return (s, y * NZ + (z + d + NZ) % NZ)

    def ydev(d):
        return (s, ((y + d) % NY) * NZ + z)

    def sdev(d):
        return ((s + d) % NS, ch)

    def send(src, dst, ss, rs, dev):
        c = pltpu.make_async_remote_copy(
            src_ref=src, dst_ref=dst, send_sem=ss, recv_sem=rs, device_id=dev, device_id_type=MESH
        )
        c.start()
        return c

    near = ((0, -1), (2, 1), (3, 2))

    barrier = pltpu.get_barrier_semaphore()
    peers = [sdev(d) for d in range(1, NS)] + [ydev(d) for d in range(1, NY)]
    peers += [zdev(4 * k) for k in range(1, 8)] + [zdev(d) for d in (-2, -1, 1, 2)]
    for dev in peers:
        pl.semaphore_signal(barrier, inc=1, device_id=dev, device_id_type=MESH)


    key_value = x_ref[1].astype(jnp.float32) * x_ref[2].astype(jnp.float32)
    kv[...] = key_value.astype(jnp.bfloat16).reshape(NS, 2, 16, 128)
    for c in range(2):
        xp[c, 0:16, :] = jnp.zeros((16, 128), jnp.float32)
        xp[c, 144:160, :] = jnp.zeros((16, 128), jnp.float32)
    pl.semaphore_wait(barrier, len(peers))

    c_hx = [
        send(h_ref.at[(s + d) % NS], hx.at[d - 1], s_hx.at[d], r_hx.at[d], sdev(d))
        for d in range(1, NS)
    ]
    c_kv = [
        send(kv.at[(s + d) % NS], rx.at[d], s_kv.at[d], r_kv.at[d], sdev(d)) for d in range(1, NS)
    ]
    c_wa = [send(w_ref.at[:, m], wa.at[m], s_wa.at[m], r_wa.at[m], zdev(o)) for m, o in near]
    own_wa = pltpu.make_async_copy(w_ref.at[:, 1], wa.at[1], s_loc.at[0])
    own_wa.start()
    for c in c_hx:
        c.wait_recv()

    def put_taps(d, block):
        a = pl.multiple_of((s + NS - d) % NS * 16, 16)
        for c in range(2):
            hf[c, pl.ds(a, 16), :] = block[c].astype(jnp.float32)

    put_taps(0, h_ref[s])
    for d in range(1, NS):
        put_taps(d, hx[d - 1])

    row = lax.broadcasted_iota(jnp.int32, (128, 128), 0)
    col = lax.broadcasted_iota(jnp.int32, (128, 128), 1)
    upper = col >= row

    def taps_blocks(c):
        def body(d, last):
            line = jnp.broadcast_to(hf[c, pl.ds(d, 1), :], (128, 128))
            now = pltpu.roll(line, 0, 1, stride=1, stride_axis=0)
            tt[c, d] = jnp.where(upper, now, last).astype(jnp.bfloat16)
            return now

        lax.fori_loop(0, 128, body, jnp.zeros((128, 128), jnp.float32), unroll=4)

    taps_blocks(0)
    own_wa.wait()
    for c in c_wa:
        c.wait_recv()
    c_wb = [
        send(wa.at[:, k], wg.at[0, k], s_wb.at[k], r_wb.at[k], zdev(4 * k)) for k in range(1, 8)
    ]
    own_wb = pltpu.make_async_copy(wa.at[:, 0], wg.at[0, 0], s_loc.at[1])
    own_wb.start()
    taps_blocks(1)

    def place(blocks):
        for a in range(NS):
            for c in range(2):
                xp[c, 16 + 16 * a : 32 + 16 * a, :] = blocks[(s + NS - a) % NS, c].astype(
                    jnp.float32
                )

    for c in c_kv:
        c.wait_recv()
    rx[0] = kv[s]
    place(rx)

    def forward(c, carry):
        for d in range(16):
            sh[:, 128 * d : 128 * d + 128] = xp[c, 16 - d : 144 - d, :].astype(jnp.bfloat16)
        for p in range(4):
            taps = jnp.concatenate(
                [tt[c, 32 * p + 16 * h : 32 * p + 16 * h + 16].reshape(2048, 128) for h in range(2)],
                axis=1,
            )
            rows = 128 - 32 * p
            part = jnp.dot(sh[0:rows, :], taps, preferred_element_type=jnp.float32)
            first = part[:, :128].reshape(8 - 2 * p, 16, 128)
            second = part[: rows - 16, 128:].reshape(7 - 2 * p, 16, 128)
            if p == 0:
                yy[c] = first
            else:
                yy[c, 2 * p : 8] = yy[c, 2 * p : 8] + first
            yy[c, 2 * p + 1 : 8] = yy[c, 2 * p + 1 : 8] + second
        return carry

    lax.fori_loop(0, 2, forward, 0)
    c_cv = [
        send(yy.at[:, (s + d) % NS], cv.at[d], s_cv.at[d], r_cv.at[d], sdev(d))
        for d in range(1, NS)
    ]
    cv[0] = yy[:, s]
    own_wb.wait()
    for c in c_wb:
        c.wait_recv()
    c_wy = [
        send(wg.at[0], wg.at[d], s_wy.at[d], r_wy.at[d], ydev(d)) for d in range(1, NY)
    ]
    for c in c_cv:
        c.wait_recv()

    def collect(blocks):
        return jnp.concatenate(
            [blocks[(s + NS - a) % NS].reshape(32, 128) for a in range(NS)], axis=0
        )

    skip = skip_ref[...]
    query = x_ref[0].astype(jnp.float32)
    mixed = collect(cv) + skip * key_value
    oo[...] = query * mixed
    out_ref[0] = mixed

    small_row = lax.broadcasted_iota(jnp.int32, (16, 128), 0)
    small_col = lax.broadcasted_iota(jnp.int32, (16, 128), 1)
    spread = [
        jnp.where(
            (small_row // 4 == j) & (small_col // 32 == small_row % 4), 1.0 / POOL, 0.0
        ).astype(jnp.bfloat16)
        for j in range(4)
    ]

    def halves(val):
        top = val.astype(jnp.bfloat16)
        return top, (val - top.astype(jnp.float32)).astype(jnp.bfloat16)

    nt = (((1,), (1,)), ((), ()))
    nn = (((1,), (0,)), ((), ()))
    for d in range(NY):
        mean = jnp.zeros((16, 16), jnp.float32)
        for j in range(4):
            rows = oo[pl.ds((y + d) % NY * 4 + j, 16, stride=16), :]
            for piece in halves(rows):
                mean = mean + lax.dot_general(
                    spread[j], piece, nt, preferred_element_type=jnp.float32
                )
        lanes_of = (small_col == small_row + 16 * d).astype(jnp.float32).astype(jnp.bfloat16)
        pp[d] = lax.dot_general(
            mean.astype(jnp.bfloat16), lanes_of, nn, preferred_element_type=jnp.float32
        ).astype(jnp.bfloat16)
    c_py = [
        send(pp.at[d], py.at[d - 1], s_py.at[d], r_py.at[d], ydev(d)) for d in range(1, NY)
    ]
    for c in c_py:
        c.wait_recv()
    tile = pp[0].astype(jnp.float32)
    for d in range(NY - 1):
        tile = tile + py[d].astype(jnp.float32)
    pg[1, 0] = tile.astype(jnp.bfloat16)
    c_pf = [
        send(pg.at[1, 0], pg.at[1, k], s_pf.at[k], r_pf.at[k], zdev(4 * k)) for k in range(1, 8)
    ]
    for c in c_pf:
        c.wait_recv()
    c_pn = [send(pg.at[1], pg.at[m], s_pn.at[m], r_pn.at[m], zdev(o)) for m, o in near]

    for c in c_pn:
        c.wait_recv()
    for c in c_wy:
        c.wait_recv()

    logits = jnp.broadcast_to(bias_ref[0:1, :], (16, 128))
    for k in range(8):
        for m in range(4):
            rows = jnp.concatenate([wg[d, k, m] for d in range(NY)], axis=0)
            logits = logits + lax.dot_general(
                pg[m, k][:, :64], rows, (((1,), (0,)), ((), ())),
                preferred_element_type=jnp.float32,
            )
    rates = jnp.maximum(logits, 0.0) + jnp.log1p(jnp.exp(-jnp.abs(logits))) + rate_floor
    observed = cnt_ref[...].astype(jnp.float32)
    part = [
        jnp.sum(rates, axis=0, keepdims=True),
        jnp.sum(observed, axis=0, keepdims=True),
        jnp.sum(observed * jnp.log(rates), axis=0, keepdims=True),
        jnp.zeros((5, 128), jnp.float32),
    ]
    ty[0] = jnp.concatenate(part, axis=0)
    c_ty = [send(ty.at[0], ty.at[d], s_ty.at[d], r_ty.at[d], ydev(d)) for d in range(1, NY)]
    sig = 1.0 / (1.0 + jnp.exp(-logits))
    obs_rate = observed / rates
    for c in c_ty:
        c.wait_recv()
    tot = ty[y]
    for a in range(1, NY):
        tot = tot + ty[(y + NY - a) % NY]
    ts[0] = tot
    c_ts = [send(ts.at[0], ts.at[d], s_ts.at[d], r_ts.at[d], sdev(d)) for d in range(1, NS)]
    for c in c_ts:
        c.wait_recv()
    tot = ts[s]
    for a in range(1, NS):
        tot = tot + ts[(s + NS - a) % NS]
    pred = tot[0:1, :]
    obs = tot[1:2, :]
    log_pred = jnp.log(pred)
    lane = lax.broadcasted_iota(jnp.int32, (1, 128), 1)
    terms = total_weight * (pred - obs * log_pred) + obs * log_pred - tot[2:3, :]
    loss = jnp.sum(jnp.where(lane < TR, terms, 0.0), axis=1, keepdims=True)
    ratio = obs / pred
    grad_rates = total_weight * (1.0 - ratio) + ratio - obs_rate
    grad = grad_rates * sig
    hi = loss.astype(jnp.bfloat16).astype(jnp.float32)
    mid = (loss - hi).astype(jnp.bfloat16).astype(jnp.float32)
    lo = loss - hi - mid
    lanes = lax.broadcasted_iota(jnp.int32, (16, 128), 1)
    grad = jnp.where(
        lanes < TR, grad, jnp.where(lanes == TR, hi, jnp.where(lanes == TR + 1, mid, lo))
    )
    gg[0, 1, 0] = grad.astype(jnp.bfloat16)
    c_gf = [
        send(gg.at[0, 1, 0], gg.at[0, 1, k], s_gf.at[k], r_gf.at[k], zdev(-4 * k))
        for k in range(1, 8)
    ]
    for c in c_gf:
        c.wait_recv()
    c_gn = [
        send(gg.at[0, 1], gg.at[0, m], s_gn.at[m], r_gn.at[m], zdev(-o)) for m, o in near
    ]
    c_gy = [
        send(gg.at[0, 1], gg.at[d, 1], s_gy.at[d, 1], r_gy.at[d, 1], ydev(d))
        for d in range(1, NY)
    ]
    for c, (m, o) in zip(c_gn, near):
        c.wait_recv()
        c_gy += [
            send(gg.at[0, m], gg.at[d, m], s_gy.at[d, m], r_gy.at[d, m], ydev(d))
            for d in range(1, NY)
        ]

    by_z = jnp.zeros((1, 128), jnp.float32)
    for k in range(8):
        for m in range(4):
            row = gg[0, m, k][0:1, :].astype(jnp.float32)
            val = jnp.sum(
                jnp.where((lane >= TR) & (lane < TR + 3), row, 0.0), axis=1, keepdims=True
            )
            by_z = jnp.where(lane == (z + m - 1 + 4 * k + NZ) % NZ, val, by_z)
    loss_ref[...] = jnp.broadcast_to(jnp.sum(by_z, axis=1, keepdims=True), (8, 128))


    wl = jnp.concatenate([w_ref[k, m] for k in range(8) for m in range(4)], axis=1)

    def grad_block(d):
        gl = jnp.concatenate([gg[d, m, k] for k in range(8) for m in range(4)], axis=1)
        block = lax.dot_general(wl, gl, nt, preferred_element_type=jnp.float32)
        top, low = halves(block)
        for j in range(4):
            rows = lax.dot_general(top, spread[j], nn, preferred_element_type=jnp.float32)
            rows = rows + lax.dot_general(low, spread[j], nn, preferred_element_type=jnp.float32)
            oo[pl.ds((y + NY - d) % NY * 4 + j, 16, stride=16), :] = rows

    grad_block(0)
    for c in c_gy:
        c.wait_recv()
    for d in range(1, NY):
        grad_block(d)

    gated = oo[...] * query
    gg_out[...] = gated.astype(jnp.bfloat16).reshape(NS, 2, 16, 128)
    c_gx = [
        send(gg_out.at[(s + d) % NS], gx.at[d], s_gx.at[d], r_gx.at[d], sdev(d))
        for d in range(1, NS)
    ]
    gx[0] = gg_out[s]
    out_ref[0] = oo[...] * out_ref[0]
    for c in c_cv:
        c.wait_send()
    for c in c_gx:
        c.wait_recv()
    place(gx)

    def backward(c, carry):
        for d in range(16):
            sh[:, 128 * d : 128 * d + 128] = xp[c, 16 + d : 144 + d, :].astype(jnp.bfloat16)
        for p in range(4):
            taps = jnp.concatenate(
                [
                    jnp.concatenate([tt[c, 32 * p + 16 * h + e] for e in range(16)], axis=1)
                    for h in range(2)
                ],
                axis=0,
            )
            rows = 128 - 32 * p
            part = lax.dot_general(
                sh[32 * p : 128, :], taps, nt, preferred_element_type=jnp.float32
            )
            first = part[:, :128].reshape(8 - 2 * p, 16, 128)
            second = part[16:, 128:].reshape(7 - 2 * p, 16, 128)
            if p == 0:
                yy[c] = first
            else:
                yy[c, 0 : 8 - 2 * p] = yy[c, 0 : 8 - 2 * p] + first
            yy[c, 0 : 7 - 2 * p] = yy[c, 0 : 7 - 2 * p] + second
        return carry

    lax.fori_loop(0, 2, backward, 0)
    c_gr = [
        send(yy.at[:, (s + d) % NS], gr.at[d], s_gr.at[d], r_gr.at[d], sdev(d))
        for d in range(1, NS)
    ]
    gr[0] = yy[:, s]
    for c in c_gr:
        c.wait_recv()
    grad_kv = collect(gr) + skip * (oo[...] * query)
    out_ref[1] = grad_kv * x_ref[2].astype(jnp.float32)
    out_ref[2] = grad_kv * x_ref[1].astype(jnp.float32)

    for c in c_hx + c_kv + c_wa + c_py + c_wb + c_pf + c_pn + c_wy + c_ty + c_ts:
        c.wait_send()
    for c in c_gf + c_gn + c_gy + c_gx + c_gr:
        c.wait_send()


def per_device(projections, filter_taps, skip_gain, head_weight, head_bias, counts):
    ch = lax.axis_index("chan")
    y = ch // NZ
    z = ch % NZ
    x = projections.reshape(3, 256, 128)
    h = filter_taps.astype(jnp.bfloat16).reshape(NS, 2, 16, 128)
    skip = jnp.broadcast_to(skip_gain[:, None], (16, 16)).reshape(256, 1)
    w = jnp.pad(head_weight.reshape(16, NZ, TR), ((0, 0), (0, 0), (0, 128 - TR)))
    w = jnp.transpose(w, (1, 0, 2))
    w = lax.dynamic_slice_in_dim(jnp.concatenate([w, w], axis=0), (z + NZ - 1) % NZ, NZ, 0)
    w = w.reshape(8, 4, 16, 128)
    cnt = lax.dynamic_slice(counts, (y * 16, z * TR), (16, TR))
    cnt = jnp.pad(cnt, ((0, 0), (0, 128 - TR)))
    bias = jnp.pad(lax.dynamic_slice_in_dim(head_bias, z * TR, TR, 0), (0, 128 - TR))
    bias = jnp.broadcast_to(bias[None, :], (8, 128))
    sem = pltpu.SemaphoreType.DMA
    b16 = jnp.bfloat16
    f32 = jnp.float32
    out, loss = pl.pallas_call(
        step_kernel,
        out_shape=(
            jax.ShapeDtypeStruct((3, 256, 128), f32),
            jax.ShapeDtypeStruct((8, 128), f32),
        ),
        in_specs=[pl.BlockSpec(memory_space=pltpu.VMEM)] * 6,
        out_specs=(pl.BlockSpec(memory_space=pltpu.VMEM),) * 2,
        scratch_shapes=[
            pltpu.VMEM((8, 2, 16, 128), b16),
            pltpu.VMEM((7, 2, 16, 128), b16),
            pltpu.VMEM((8, 2, 16, 128), b16),
            pltpu.VMEM((2, 160, 128), f32),
            pltpu.VMEM((2, 128, 128), f32),
            pltpu.VMEM((128, 2048), b16),
            pltpu.VMEM((2, 128, 128, 128), b16),
            pltpu.VMEM((2, 8, 16, 128), f32),
            pltpu.VMEM((8, 2, 16, 128), f32),
            pltpu.VMEM((256, 128), f32),
            pltpu.VMEM((8, 2, 16, 128), b16),
            pltpu.VMEM((8, 2, 16, 128), b16),
            pltpu.VMEM((8, 2, 16, 128), f32),
            pltpu.VMEM((4, 16, 128), b16),
            pltpu.VMEM((4, 8, 16, 128), b16),
            pltpu.VMEM((4, 8, 4, 16, 128), b16),
            pltpu.VMEM((3, 16, 128), b16),
            pltpu.VMEM((4, 8, 16, 128), b16),
            pltpu.VMEM((4, 8, 128), f32),
            pltpu.VMEM((8, 8, 128), f32),
            pltpu.VMEM((4, 4, 8, 16, 128), b16),
            sem((2,)),
            sem((8,)), sem((8,)), sem((8,)), sem((8,)), sem((8,)), sem((8,)),
            sem((8,)), sem((8,)), sem((8,)), sem((8,)),
            sem((4,)), sem((4,)), sem((8,)), sem((8,)), sem((4,)), sem((4,)),
            sem((4,)), sem((4,)), sem((8,)), sem((8,)), sem((4,)), sem((4,)),
            sem((4,)), sem((4,)), sem((8,)), sem((8,)), sem((8,)), sem((8,)),
            sem((4,)), sem((4,)), sem((4, 4)), sem((4, 4)),
        ],
        compiler_params=pltpu.CompilerParams(collective_id=0, has_side_effects=True),
    )(x, h, skip, w, cnt, bias)
    mean_loss = loss[0, 0] / (512 * 3840)
    return mean_loss, out.reshape(3, 16, 2048)


def solution(mesh):
    placed = (
        P(None, "chan", "seq"),
        P("chan", "seq"),
        P("chan"),
        P("chan", None),
        P(),
        P("seq", None),
    )
    return jax.shard_map(
        per_device,
        mesh=mesh,
        in_specs=placed,
        out_specs=(P(), P(None, "chan", "seq")),
        check_vma=False,
    )
```

```python
import jax
import jax.numpy as jnp
from jax import lax
from jax.experimental import pallas as pl
from jax.experimental.pallas import tpu as pltpu
from jax.sharding import PartitionSpec as P

POOL = 32
NY = 4
NZ = 32
NS = 8
TR = 120
FAR = (0, 1, 7, 2, 6, 3, 5, 4)
GROUPS = ((0, 3), (3, 2), (5, 2), (7, 1))
MESH = pl.DeviceIdType.MESH

total_weight = 0.2
rate_floor = 0.5


def step_kernel(
    x_ref, h_ref, skip_ref, w_ref, cnt_ref, bias_ref,
    out_ref, loss_ref,
    kv, hx, rx, xp, hf, vf, vb, pick, sh, tt, yy, yb, cv, oo, gx, gg_out, gr, pp,
    wa, wg, py, pg, ty, ts, gg,
    s_loc, s_kv, r_kv, s_hx, r_hx, s_cv, r_cv, s_gx, r_gx, s_gr, r_gr,
    s_wa, r_wa, s_wb, r_wb, s_wy, r_wy, s_py, r_py, s_pf, r_pf, s_pn, r_pn,
    s_ty, r_ty, s_ts, r_ts, s_gf, r_gf, s_gn, r_gn, s_gy, r_gy,
):
    s = lax.axis_index("seq")
    ch = lax.axis_index("chan")
    y = ch // NZ
    z = ch % NZ

    def zdev(d):
        return (s, y * NZ + (z + d + NZ) % NZ)

    def ydev(d):
        return (s, ((y + d) % NY) * NZ + z)

    def sdev(d):
        return ((s + d) % NS, ch)

    def send(src, dst, ss, rs, dev):
        c = pltpu.make_async_remote_copy(
            src_ref=src, dst_ref=dst, send_sem=ss, recv_sem=rs, device_id=dev, device_id_type=MESH
        )
        c.start()
        return c

    near = ((0, -1), (2, 1), (3, 2))

    barrier = pltpu.get_barrier_semaphore()
    peers = [sdev(d) for d in range(1, NS)] + [ydev(d) for d in range(1, NY)]
    peers += [zdev(4 * k) for k in range(1, 8)] + [zdev(d) for d in (-2, -1, 1, 2)]
    for dev in peers:
        pl.semaphore_signal(barrier, inc=1, device_id=dev, device_id_type=MESH)


    key_value = x_ref[1].astype(jnp.float32) * x_ref[2].astype(jnp.float32)
    kv[...] = key_value.astype(jnp.bfloat16).reshape(NS, 2, 16, 128)
    for c in range(2):
        xp[c, 0:16, :] = jnp.zeros((16, 128), jnp.float32)
        xp[c, 144:160, :] = jnp.zeros((16, 128), jnp.float32)
        vf[c, 0:8, :] = jnp.zeros((8, 128), jnp.float32)
    tall = lax.broadcasted_iota(jnp.int32, (256, 256), 0)
    wide = lax.broadcasted_iota(jnp.int32, (256, 256), 1)
    for q in range(8):
        pick[q] = jnp.where(
            tall == 128 + wide % 128 - 16 * q - 8 * (wide // 128), 1.0, 0.0
        ).astype(jnp.bfloat16)
    pl.semaphore_wait(barrier, len(peers))

    c_hx = [
        send(h_ref.at[(s + d) % NS], hx.at[d - 1], s_hx.at[d], r_hx.at[d], sdev(d))
        for d in range(1, NS)
    ]
    c_kv = [
        send(kv.at[(s + d) % NS], rx.at[d], s_kv.at[d], r_kv.at[d], sdev(d)) for d in range(1, NS)
    ]
    c_wa = [send(w_ref.at[:, m], wa.at[m], s_wa.at[m], r_wa.at[m], zdev(o)) for m, o in near]
    own_wa = pltpu.make_async_copy(w_ref.at[:, 1], wa.at[1], s_loc.at[0])
    own_wa.start()
    for c in c_hx:
        c.wait_recv()

    own_wa.wait()
    for c in c_wa:
        c.wait_recv()
    c_wb = [
        send(wa.at[:, FAR[e]], wg.at[0, e], s_wb.at[e], r_wb.at[e], zdev(4 * FAR[e]))
        for e in range(7, 0, -1)
    ][::-1]
    own_wb = pltpu.make_async_copy(wa.at[:, 0], wg.at[0, 0], s_loc.at[1])
    own_wb.start()

    def put_taps(d, block):
        a = pl.multiple_of((s + NS - d) % NS * 16, 16)
        for c in range(2):
            hf[c, pl.ds(a, 16), :] = block[c].astype(jnp.float32)

    put_taps(0, h_ref[s])
    for d in range(1, NS):
        put_taps(d, hx[d - 1])

    lane8 = lax.broadcasted_iota(jnp.int32, (8, 128), 1)
    sub8 = lax.broadcasted_iota(jnp.int32, (8, 128), 0)

    def windows(c):
        def body(d, last):
            line = jnp.broadcast_to(hf[c, pl.ds(d, 1), :], (8, 128))
            now = pltpu.roll(line, 0, 1, stride=1, stride_axis=0)
            vf[c, pl.ds(pl.multiple_of(8 + 8 * d, 8), 8), :] = jnp.where(
                lane8 >= sub8, now, last
            )
            return now

        lax.fori_loop(0, 128, body, jnp.zeros((8, 128), jnp.float32), unroll=16)
        vb[c, :, 0:128] = vf[c, 0:1024, :].astype(jnp.bfloat16)
        vb[c, :, 128:256] = vf[c, 8:1032, :].astype(jnp.bfloat16)

    windows(0)
    windows(1)

    def fill(q, carry):
        for c in range(2):
            block = jnp.dot(vb[c], pick[q], preferred_element_type=jnp.float32)
            both = jnp.concatenate(
                [block[:, :128].reshape(128, 8, 128), block[:, 128:].reshape(128, 8, 128)], axis=1
            )
            tt[c, :, pl.ds(pl.multiple_of(16 * q, 16), 16), :] = both.astype(jnp.bfloat16)
        return carry

    lax.fori_loop(0, 8, fill, 0)

    def place(blocks):
        for a in range(NS):
            for c in range(2):
                xp[c, 16 + 16 * a : 32 + 16 * a, :] = blocks[(s + NS - a) % NS, c].astype(
                    jnp.float32
                )

    for c in c_kv:
        c.wait_recv()
    rx[0] = kv[s]
    place(rx)

    def forward(c, carry):
        for d in range(16):
            sh[:, 128 * d : 128 * d + 128] = xp[c, 16 - d : 144 - d, :].astype(jnp.bfloat16)
        for p in range(4):
            taps = jnp.concatenate(
                [tt[c, 32 * p + 16 * h : 32 * p + 16 * h + 16].reshape(2048, 128) for h in range(2)],
                axis=1,
            )
            rows = 128 - 32 * p
            part = jnp.dot(sh[0:rows, :], taps, preferred_element_type=jnp.float32)
            first = part[:, :128].reshape(8 - 2 * p, 16, 128)
            second = part[: rows - 16, 128:].reshape(7 - 2 * p, 16, 128)
            if p == 0:
                yy[c] = first
            else:
                yy[c, 2 * p : 8] = yy[c, 2 * p : 8] + first
            yy[c, 2 * p + 1 : 8] = yy[c, 2 * p + 1 : 8] + second
        return carry

    lax.fori_loop(0, 2, forward, 0)
    yb[...] = yy[...].astype(jnp.bfloat16)
    c_cv = [
        send(yb.at[:, (s + d) % NS], cv.at[d], s_cv.at[d], r_cv.at[d], sdev(d))
        for d in range(1, NS)
    ]
    cv[0] = yb[:, s]
    for c in c_cv:
        c.wait_recv()

    def collect(blocks):
        return jnp.concatenate(
            [blocks[(s + NS - a) % NS].astype(jnp.float32).reshape(32, 128) for a in range(NS)], axis=0
        )

    skip = skip_ref[...]
    query = x_ref[0].astype(jnp.float32)
    mixed = collect(cv) + skip * key_value
    oo[...] = query * mixed
    out_ref[0] = mixed

    small_row = lax.broadcasted_iota(jnp.int32, (16, 128), 0)
    small_col = lax.broadcasted_iota(jnp.int32, (16, 128), 1)
    spread = [
        jnp.where(
            (small_row // 4 == j) & (small_col // 32 == small_row % 4), 1.0 / POOL, 0.0
        ).astype(jnp.bfloat16)
        for j in range(4)
    ]

    def halves(val):
        top = val.astype(jnp.bfloat16)
        return top, (val - top.astype(jnp.float32)).astype(jnp.bfloat16)

    nt = (((1,), (1,)), ((), ()))
    nn = (((1,), (0,)), ((), ()))
    for d in range(NY):
        mean = jnp.zeros((16, 16), jnp.float32)
        for j in range(4):
            rows = oo[pl.ds((y + d) % NY * 4 + j, 16, stride=16), :]
            for piece in halves(rows):
                mean = mean + lax.dot_general(
                    spread[j], piece, nt, preferred_element_type=jnp.float32
                )
        lanes_of = (small_col == small_row + 16 * d).astype(jnp.float32).astype(jnp.bfloat16)
        pp[d] = lax.dot_general(
            mean.astype(jnp.bfloat16), lanes_of, nn, preferred_element_type=jnp.float32
        ).astype(jnp.bfloat16)
    c_py = [
        send(pp.at[d], py.at[d - 1], s_py.at[d], r_py.at[d], ydev(d)) for d in range(1, NY)
    ]
    for c in c_py:
        c.wait_recv()
    tile = pp[0].astype(jnp.float32)
    for d in range(NY - 1):
        tile = tile + py[d].astype(jnp.float32)
    pg[1, 0] = tile.astype(jnp.bfloat16)
    c_pf = [
        send(pg.at[1, 0], pg.at[1, e], s_pf.at[e], r_pf.at[e], zdev(4 * FAR[e]))
        for e in range(7, 0, -1)
    ][::-1]
    own_wb.wait()
    c_pn = []
    c_wy = []
    for g, (e, n) in enumerate(GROUPS):
        for c in c_pf[max(e, 1) - 1 : e + n - 1]:
            c.wait_recv()
        c_pn += [
            send(pg.at[1, e : e + n], pg.at[m, e : e + n], s_pn.at[m, g], r_pn.at[m, g], zdev(o))
            for m, o in near
        ]
        for c in c_wb[max(e, 1) - 1 : e + n - 1]:
            c.wait_recv()
        c_wy += [
            send(wg.at[0, e : e + n], wg.at[d, e : e + n], s_wy.at[d, g], r_wy.at[d, g], ydev(d))
            for d in range(1, NY)
        ]
    for c in c_pn:
        c.wait_recv()
    for c in c_wy:
        c.wait_recv()

    logits = jnp.broadcast_to(bias_ref[0:1, :], (16, 128))
    for k in range(8):
        for m in range(4):
            rows = jnp.concatenate([wg[d, k, m] for d in range(NY)], axis=0)
            logits = logits + lax.dot_general(
                pg[m, k][:, :64], rows, (((1,), (0,)), ((), ())),
                preferred_element_type=jnp.float32,
            )
    rates = jnp.maximum(logits, 0.0) + jnp.log1p(jnp.exp(-jnp.abs(logits))) + rate_floor
    observed = cnt_ref[...].astype(jnp.float32)
    part = [
        jnp.sum(rates, axis=0, keepdims=True),
        jnp.sum(observed, axis=0, keepdims=True),
        jnp.sum(observed * jnp.log(rates), axis=0, keepdims=True),
        jnp.zeros((5, 128), jnp.float32),
    ]
    ty[0] = jnp.concatenate(part, axis=0)
    c_ty = [send(ty.at[0], ty.at[d], s_ty.at[d], r_ty.at[d], ydev(d)) for d in range(1, NY)]
    sig = 1.0 / (1.0 + jnp.exp(-logits))
    obs_rate = observed / rates
    for c in c_ty:
        c.wait_recv()
    tot = ty[y]
    for a in range(1, NY):
        tot = tot + ty[(y + NY - a) % NY]
    ts[0] = tot
    c_ts = [send(ts.at[0], ts.at[d], s_ts.at[d], r_ts.at[d], sdev(d)) for d in range(1, NS)]
    for c in c_ts:
        c.wait_recv()
    tot = ts[s]
    for a in range(1, NS):
        tot = tot + ts[(s + NS - a) % NS]
    pred = tot[0:1, :]
    obs = tot[1:2, :]
    log_pred = jnp.log(pred)
    lane = lax.broadcasted_iota(jnp.int32, (1, 128), 1)
    terms = total_weight * (pred - obs * log_pred) + obs * log_pred - tot[2:3, :]
    loss = jnp.sum(jnp.where(lane < TR, terms, 0.0), axis=1, keepdims=True)
    ratio = obs / pred
    grad_rates = total_weight * (1.0 - ratio) + ratio - obs_rate
    grad = grad_rates * sig
    hi = loss.astype(jnp.bfloat16).astype(jnp.float32)
    mid = (loss - hi).astype(jnp.bfloat16).astype(jnp.float32)
    lo = loss - hi - mid
    lanes = lax.broadcasted_iota(jnp.int32, (16, 128), 1)
    grad = jnp.where(
        lanes < TR, grad, jnp.where(lanes == TR, hi, jnp.where(lanes == TR + 1, mid, lo))
    )
    gg[0, 1, 0] = grad.astype(jnp.bfloat16)
    c_gf = [
        send(gg.at[0, 1, 0], gg.at[0, 1, e], s_gf.at[e], r_gf.at[e], zdev(-4 * FAR[e]))
        for e in range(7, 0, -1)
    ][::-1]
    c_gn = []
    c_gy = []

    def over_y(m, g):
        e, n = GROUPS[g]
        return [
            send(
                gg.at[0, m, e : e + n], gg.at[d, m, e : e + n], s_gy.at[d, m, g],
                r_gy.at[d, m, g], ydev(d),
            )
            for d in range(1, NY)
        ]

    for g in range(5):
        if g < 4:
            e, n = GROUPS[g]
            for c in c_gf[max(e, 1) - 1 : e + n - 1]:
                c.wait_recv()
            c_gn.append(
                [
                    send(
                        gg.at[0, 1, e : e + n], gg.at[0, m, e : e + n], s_gn.at[m, g],
                        r_gn.at[m, g], zdev(-o),
                    )
                    for m, o in near
                ]
            )
            c_gy += over_y(1, g)
        if g > 0:
            for c, (m, o) in zip(c_gn[g - 1], near):
                c.wait_recv()
                c_gy += over_y(m, g - 1)
    c_gn = [c for some in c_gn for c in some]

    by_z = jnp.zeros((1, 128), jnp.float32)
    for k in range(8):
        for m in range(4):
            row = gg[0, m, k][0:1, :].astype(jnp.float32)
            val = jnp.sum(
                jnp.where((lane >= TR) & (lane < TR + 3), row, 0.0), axis=1, keepdims=True
            )
            by_z = jnp.where(lane == (z + m - 1 + 4 * FAR[k] + NZ) % NZ, val, by_z)
    loss_ref[...] = jnp.broadcast_to(jnp.sum(by_z, axis=1, keepdims=True), (8, 128))


    wl = jnp.concatenate([w_ref[FAR[k], m] for k in range(8) for m in range(4)], axis=1)

    def grad_block(d):
        gl = jnp.concatenate([gg[d, m, k] for k in range(8) for m in range(4)], axis=1)
        block = lax.dot_general(wl, gl, nt, preferred_element_type=jnp.float32)
        top, low = halves(block)
        for j in range(4):
            rows = lax.dot_general(top, spread[j], nn, preferred_element_type=jnp.float32)
            rows = rows + lax.dot_general(low, spread[j], nn, preferred_element_type=jnp.float32)
            oo[pl.ds((y + NY - d) % NY * 4 + j, 16, stride=16), :] = rows

    grad_block(0)
    for c in c_gy:
        c.wait_recv()
    for d in range(1, NY):
        grad_block(d)

    gated = oo[...] * query
    gg_out[...] = gated.astype(jnp.bfloat16).reshape(NS, 2, 16, 128)
    c_gx = [
        send(gg_out.at[(s + d) % NS], gx.at[d], s_gx.at[d], r_gx.at[d], sdev(d))
        for d in range(1, NS)
    ]
    gx[0] = gg_out[s]
    out_ref[0] = oo[...] * out_ref[0]
    for c in c_cv:
        c.wait_send()
    for c in c_gx:
        c.wait_recv()
    place(gx)

    def backward(c, carry):
        for d in range(16):
            sh[:, 128 * d : 128 * d + 128] = xp[c, 16 + d : 144 + d, :].astype(jnp.bfloat16)
        for p in range(4):
            taps = jnp.concatenate(
                [
                    jnp.concatenate([tt[c, 32 * p + 16 * h + e] for e in range(16)], axis=1)
                    for h in range(2)
                ],
                axis=0,
            )
            rows = 128 - 32 * p
            part = lax.dot_general(
                sh[32 * p : 128, :], taps, nt, preferred_element_type=jnp.float32
            )
            first = part[:, :128].reshape(8 - 2 * p, 16, 128)
            second = part[16:, 128:].reshape(7 - 2 * p, 16, 128)
            if p == 0:
                yy[c] = first
            else:
                yy[c, 0 : 8 - 2 * p] = yy[c, 0 : 8 - 2 * p] + first
            yy[c, 0 : 7 - 2 * p] = yy[c, 0 : 7 - 2 * p] + second
        return carry

    lax.fori_loop(0, 2, backward, 0)
    yb[...] = yy[...].astype(jnp.bfloat16)
    c_gr = [
        send(yb.at[:, (s + d) % NS], gr.at[d], s_gr.at[d], r_gr.at[d], sdev(d))
        for d in range(1, NS)
    ]
    gr[0] = yb[:, s]
    for c in c_gr:
        c.wait_recv()
    grad_kv = collect(gr) + skip * (oo[...] * query)
    out_ref[1] = grad_kv * x_ref[2].astype(jnp.float32)
    out_ref[2] = grad_kv * x_ref[1].astype(jnp.float32)

    for c in c_hx + c_kv + c_wa + c_py + c_wb + c_pf + c_pn + c_wy + c_ty + c_ts:
        c.wait_send()
    for c in c_gf + c_gn + c_gy + c_gx + c_gr:
        c.wait_send()


def per_device(projections, filter_taps, skip_gain, head_weight, head_bias, counts):
    ch = lax.axis_index("chan")
    y = ch // NZ
    z = ch % NZ
    x = projections.reshape(3, 256, 128)
    h = filter_taps.astype(jnp.bfloat16).reshape(NS, 2, 16, 128)
    skip = jnp.broadcast_to(skip_gain[:, None], (16, 16)).reshape(256, 1)
    w = jnp.pad(head_weight.reshape(16, NZ, TR), ((0, 0), (0, 0), (0, 128 - TR)))
    w = jnp.transpose(w, (1, 0, 2))
    w = lax.dynamic_slice_in_dim(jnp.concatenate([w, w], axis=0), (z + NZ - 1) % NZ, NZ, 0)
    w = w.reshape(8, 4, 16, 128)
    cnt = lax.dynamic_slice(counts, (y * 16, z * TR), (16, TR))
    cnt = jnp.pad(cnt, ((0, 0), (0, 128 - TR)))
    bias = jnp.pad(lax.dynamic_slice_in_dim(head_bias, z * TR, TR, 0), (0, 128 - TR))
    bias = jnp.broadcast_to(bias[None, :], (8, 128))
    sem = pltpu.SemaphoreType.DMA
    b16 = jnp.bfloat16
    f32 = jnp.float32
    out, loss = pl.pallas_call(
        step_kernel,
        out_shape=(
            jax.ShapeDtypeStruct((3, 256, 128), f32),
            jax.ShapeDtypeStruct((8, 128), f32),
        ),
        in_specs=[pl.BlockSpec(memory_space=pltpu.VMEM)] * 6,
        out_specs=(pl.BlockSpec(memory_space=pltpu.VMEM),) * 2,
        scratch_shapes=[
            pltpu.VMEM((8, 2, 16, 128), b16),
            pltpu.VMEM((7, 2, 16, 128), b16),
            pltpu.VMEM((8, 2, 16, 128), b16),
            pltpu.VMEM((2, 160, 128), f32),
            pltpu.VMEM((2, 128, 128), f32),
            pltpu.VMEM((2, 1032, 128), f32),
            pltpu.VMEM((2, 1024, 256), b16),
            pltpu.VMEM((8, 256, 256), b16),
            pltpu.VMEM((128, 2048), b16),
            pltpu.VMEM((2, 128, 128, 128), b16),
            pltpu.VMEM((2, 8, 16, 128), f32),
            pltpu.VMEM((2, 8, 16, 128), b16),
            pltpu.VMEM((8, 2, 16, 128), b16),
            pltpu.VMEM((256, 128), f32),
            pltpu.VMEM((8, 2, 16, 128), b16),
            pltpu.VMEM((8, 2, 16, 128), b16),
            pltpu.VMEM((8, 2, 16, 128), b16),
            pltpu.VMEM((4, 16, 128), b16),
            pltpu.VMEM((4, 8, 16, 128), b16),
            pltpu.VMEM((4, 8, 4, 16, 128), b16),
            pltpu.VMEM((3, 16, 128), b16),
            pltpu.VMEM((4, 8, 16, 128), b16),
            pltpu.VMEM((4, 8, 128), f32),
            pltpu.VMEM((8, 8, 128), f32),
            pltpu.VMEM((4, 4, 8, 16, 128), b16),
            sem((2,)),
            sem((8,)), sem((8,)), sem((8,)), sem((8,)), sem((8,)), sem((8,)),
            sem((8,)), sem((8,)), sem((8,)), sem((8,)),
            sem((4,)), sem((4,)), sem((8,)), sem((8,)), sem((4, 4)), sem((4, 4)),
            sem((4,)), sem((4,)), sem((8,)), sem((8,)), sem((4, 4)), sem((4, 4)),
            sem((4,)), sem((4,)), sem((8,)), sem((8,)), sem((8,)), sem((8,)),
            sem((4, 4)), sem((4, 4)), sem((4, 4, 4)), sem((4, 4, 4)),
        ],
        compiler_params=pltpu.CompilerParams(collective_id=0, has_side_effects=True),
    )(x, h, skip, w, cnt, bias)
    mean_loss = loss[0, 0] / (512 * 3840)
    return mean_loss, out.reshape(3, 16, 2048)


def solution(mesh):
    placed = (
        P(None, "chan", "seq"),
        P("chan", "seq"),
        P("chan"),
        P("chan", None),
        P(),
        P("seq", None),
    )
    return jax.shard_map(
        per_device,
        mesh=mesh,
        in_specs=placed,
        out_specs=(P(), P(None, "chan", "seq")),
        check_vma=False,
    )
```

```python
import jax
import jax.numpy as jnp
from jax import lax
from jax.experimental import pallas as pl
from jax.experimental.pallas import tpu as pltpu
from jax.sharding import PartitionSpec as P

POOL = 32
NY = 4
NZ = 32
NS = 8
TR = 120
FAR = (0, 1, 7, 2, 6, 3, 5, 4)
GROUPS = ((0, 3), (3, 2), (5, 2), (7, 1))
MESH = pl.DeviceIdType.MESH

total_weight = 0.2
rate_floor = 0.5


def step_kernel(
    proj_ref, taps_ref, skip_ref, head_ref, count_ref, bias_ref,
    out_ref, loss_ref,
    x_ref, ht, h_ref, w_ref, cnt_ref, mx, kv, hx, rx, xp, hf, vf, vb, pick, sh, tt, yy, yb, cv, oo, gx, gg_out, gr, pp,
    wa, wg, py, pg, ty, gg,
    s_loc, s_kv, r_kv, s_hx, r_hx, s_cv, r_cv, s_gx, r_gx, s_gr, r_gr,
    s_wa, r_wa, s_wb, r_wb, s_wy, r_wy, s_py, r_py, s_pf, r_pf, s_pn, r_pn,
    s_ty, r_ty, s_gf, r_gf, s_gn, r_gn, s_gy, r_gy,
):
    s = lax.axis_index("seq")
    ch = lax.axis_index("chan")
    y = ch // NZ
    z = ch % NZ

    def zdev(d):
        return (s, y * NZ + (z + d + NZ) % NZ)

    def ydev(d):
        return (s, ((y + d) % NY) * NZ + z)

    def sdev(d):
        return ((s + d) % NS, ch)

    def both_dev(a, b):
        return ((s + b) % NS, ((y + a) % NY) * NZ + z)

    def send(src, dst, ss, rs, dev):
        c = pltpu.make_async_remote_copy(
            src_ref=src, dst_ref=dst, send_sem=ss, recv_sem=rs, device_id=dev, device_id_type=MESH
        )
        c.start()
        return c

    near = ((0, -1), (2, 1), (3, 2))

    barrier = pltpu.get_barrier_semaphore()
    group = [(a, b) for a in range(NY) for b in range(NS) if a or b]
    peers = [both_dev(a, b) for a, b in group]
    peers += [zdev(4 * k) for k in range(1, 8)] + [zdev(d) for d in (-2, -1, 1, 2)]
    for dev in peers:
        pl.semaphore_signal(barrier, inc=1, device_id=dev, device_id_type=MESH)


    base = 120 * z // 128 - z // 31
    shift = (256 - (120 * z - 128 * base)) % 256
    base = pl.multiple_of(128 * base, 128)
    c_cnt = pltpu.make_async_copy(
        count_ref.at[pl.ds(pl.multiple_of(16 * y, 16), 16), pl.ds(base, 256)], cnt_ref, s_loc.at[2]
    )
    c_cnt.start()
    for a in range(16):
        for p in range(3):
            x_ref[p, pl.ds(a, 16, stride=16), :] = proj_ref[
                p, :, 128 * a : 128 * a + 128
            ].astype(jnp.float32)
        ht[pl.ds(a, 16, stride=16), :] = taps_ref[:, 128 * a : 128 * a + 128]
    h_ref[...] = ht[...].astype(jnp.bfloat16).reshape(NS, 2, 16, 128)
    tile_lane = lax.broadcasted_iota(jnp.int32, (16, 128), 1)
    for t in range(NZ):
        first = min(TR * t // 128, 28) * 128
        tile = head_ref[:, first : first + 256].astype(jnp.float32)
        tile = pltpu.roll(tile, (256 - (TR * t - first)) % 256, 1)[:, :128]
        at = (t + NZ + 1 - z) % NZ
        w_ref[at // 4, at % 4] = jnp.where(tile_lane < TR, tile, 0.0).astype(jnp.bfloat16)
    key_value = x_ref[1] * x_ref[2]
    kv[...] = key_value.astype(jnp.bfloat16).reshape(NS, 2, 16, 128)
    for c in range(2):
        xp[c, 0:16, :] = jnp.zeros((16, 128), jnp.float32)
        xp[c, 144:160, :] = jnp.zeros((16, 128), jnp.float32)
        vf[c, 0:8, :] = jnp.zeros((8, 128), jnp.float32)
    tall = lax.broadcasted_iota(jnp.int32, (256, 256), 0)
    wide = lax.broadcasted_iota(jnp.int32, (256, 256), 1)
    for q in range(8):
        pick[q] = jnp.where(
            tall == 128 + wide % 128 - 16 * q - 8 * (wide // 128), 1.0, 0.0
        ).astype(jnp.bfloat16)
    pl.semaphore_wait(barrier, len(peers))

    c_hx = [
        send(h_ref.at[(s + d) % NS], hx.at[d - 1], s_hx.at[d], r_hx.at[d], sdev(d))
        for d in range(1, NS)
    ]
    c_kv = [
        send(kv.at[(s + d) % NS], rx.at[d], s_kv.at[d], r_kv.at[d], sdev(d)) for d in range(1, NS)
    ]
    c_wa = [send(w_ref.at[:, m], wa.at[m], s_wa.at[m], r_wa.at[m], zdev(o)) for m, o in near]
    own_wa = pltpu.make_async_copy(w_ref.at[:, 1], wa.at[1], s_loc.at[0])
    own_wa.start()
    for c in c_hx:
        c.wait_recv()

    own_wa.wait()
    for c in c_wa:
        c.wait_recv()
    c_wb = [
        send(wa.at[:, FAR[e]], wg.at[0, e], s_wb.at[e], r_wb.at[e], zdev(4 * FAR[e]))
        for e in range(7, 0, -1)
    ][::-1]
    own_wb = pltpu.make_async_copy(wa.at[:, 0], wg.at[0, 0], s_loc.at[1])
    own_wb.start()

    def put_taps(d, block):
        a = pl.multiple_of((s + NS - d) % NS * 16, 16)
        for c in range(2):
            hf[c, pl.ds(a, 16), :] = block[c].astype(jnp.float32)

    put_taps(0, h_ref[s])
    for d in range(1, NS):
        put_taps(d, hx[d - 1])

    lane8 = lax.broadcasted_iota(jnp.int32, (8, 128), 1)
    sub8 = lax.broadcasted_iota(jnp.int32, (8, 128), 0)

    def windows(c):
        def body(d, last):
            line = jnp.broadcast_to(hf[c, pl.ds(d, 1), :], (8, 128))
            now = pltpu.roll(line, 0, 1, stride=1, stride_axis=0)
            vf[c, pl.ds(pl.multiple_of(8 + 8 * d, 8), 8), :] = jnp.where(
                lane8 >= sub8, now, last
            )
            return now

        lax.fori_loop(0, 128, body, jnp.zeros((8, 128), jnp.float32), unroll=16)
        vb[c, :, 0:128] = vf[c, 0:1024, :].astype(jnp.bfloat16)
        vb[c, :, 128:256] = vf[c, 8:1032, :].astype(jnp.bfloat16)

    windows(0)
    windows(1)

    def fill(q, carry):
        for c in range(2):
            block = jnp.dot(vb[c], pick[q], preferred_element_type=jnp.float32)
            both = jnp.concatenate(
                [block[:, :128].reshape(128, 8, 128), block[:, 128:].reshape(128, 8, 128)], axis=1
            )
            tt[c, :, pl.ds(pl.multiple_of(16 * q, 16), 16), :] = both.astype(jnp.bfloat16)
        return carry

    lax.fori_loop(0, 8, fill, 0)

    def place(blocks):
        for a in range(NS):
            for c in range(2):
                xp[c, 16 + 16 * a : 32 + 16 * a, :] = blocks[(s + NS - a) % NS, c].astype(
                    jnp.float32
                )

    for c in c_kv:
        c.wait_recv()
    rx[0] = kv[s]
    place(rx)

    def forward(c, carry):
        for d in range(16):
            sh[:, 128 * d : 128 * d + 128] = xp[c, 16 - d : 144 - d, :].astype(jnp.bfloat16)
        for p in range(4):
            taps = jnp.concatenate(
                [tt[c, 32 * p + 16 * h : 32 * p + 16 * h + 16].reshape(2048, 128) for h in range(2)],
                axis=1,
            )
            rows = 128 - 32 * p
            part = jnp.dot(sh[0:rows, :], taps, preferred_element_type=jnp.float32)
            first = part[:, :128].reshape(8 - 2 * p, 16, 128)
            second = part[: rows - 16, 128:].reshape(7 - 2 * p, 16, 128)
            if p == 0:
                yy[c] = first
            else:
                yy[c, 2 * p : 8] = yy[c, 2 * p : 8] + first
            yy[c, 2 * p + 1 : 8] = yy[c, 2 * p + 1 : 8] + second
        return carry

    lax.fori_loop(0, 2, forward, 0)
    yb[...] = yy[...].astype(jnp.bfloat16)
    c_cv = [
        send(yb.at[:, (s + d) % NS], cv.at[d], s_cv.at[d], r_cv.at[d], sdev(d))
        for d in range(1, NS)
    ]
    cv[0] = yb[:, s]
    for c in c_cv:
        c.wait_recv()

    def collect(blocks):
        return jnp.concatenate(
            [blocks[(s + NS - a) % NS].astype(jnp.float32).reshape(32, 128) for a in range(NS)], axis=0
        )

    skip = jnp.concatenate(
        [jnp.full((16, 128), skip_ref[c], jnp.float32) for c in range(16)], axis=0
    )
    query = x_ref[0]
    mixed = collect(cv) + skip * key_value
    oo[...] = query * mixed
    mx[...] = mixed

    small_row = lax.broadcasted_iota(jnp.int32, (16, 128), 0)
    small_col = lax.broadcasted_iota(jnp.int32, (16, 128), 1)
    spread = [
        jnp.where(
            (small_row // 4 == j) & (small_col // 32 == small_row % 4), 1.0 / POOL, 0.0
        ).astype(jnp.bfloat16)
        for j in range(4)
    ]

    def halves(val):
        top = val.astype(jnp.bfloat16)
        return top, (val - top.astype(jnp.float32)).astype(jnp.bfloat16)

    nt = (((1,), (1,)), ((), ()))
    nn = (((1,), (0,)), ((), ()))
    for d in range(NY):
        mean = jnp.zeros((16, 16), jnp.float32)
        for j in range(4):
            rows = oo[pl.ds((y + d) % NY * 4 + j, 16, stride=16), :]
            for piece in halves(rows):
                mean = mean + lax.dot_general(
                    spread[j], piece, nt, preferred_element_type=jnp.float32
                )
        lanes_of = (small_col == small_row + 16 * d).astype(jnp.float32).astype(jnp.bfloat16)
        pp[d] = lax.dot_general(
            mean.astype(jnp.bfloat16), lanes_of, nn, preferred_element_type=jnp.float32
        ).astype(jnp.bfloat16)
    c_py = [
        send(pp.at[d], py.at[d - 1], s_py.at[d], r_py.at[d], ydev(d)) for d in range(1, NY)
    ]
    for c in c_py:
        c.wait_recv()
    tile = pp[0].astype(jnp.float32)
    for d in range(NY - 1):
        tile = tile + py[d].astype(jnp.float32)
    pg[1, 0] = tile.astype(jnp.bfloat16)
    c_pf = [
        send(pg.at[1, 0], pg.at[1, e], s_pf.at[e], r_pf.at[e], zdev(4 * FAR[e]))
        for e in range(7, 0, -1)
    ][::-1]
    own_wb.wait()
    c_pn = []
    c_wy = []
    for g, (e, n) in enumerate(GROUPS):
        for c in c_pf[max(e, 1) - 1 : e + n - 1]:
            c.wait_recv()
        c_pn += [
            send(pg.at[1, e : e + n], pg.at[m, e : e + n], s_pn.at[m, g], r_pn.at[m, g], zdev(o))
            for m, o in near
        ]
        for c in c_wb[max(e, 1) - 1 : e + n - 1]:
            c.wait_recv()
        c_wy += [
            send(wg.at[0, e : e + n], wg.at[d, e : e + n], s_wy.at[d, g], r_wy.at[d, g], ydev(d))
            for d in range(1, NY)
        ]
    for c in c_pn:
        c.wait_recv()
    for c in c_wy:
        c.wait_recv()

    bias = jnp.broadcast_to(bias_ref[0:1, pl.ds(base, 256)], (16, 256))
    bias = pltpu.roll(bias, shift, 1)[:, :128]
    logits = jnp.where(tile_lane < TR, bias, 0.0)
    for k in range(8):
        for m in range(4):
            rows = jnp.concatenate([wg[d, k, m] for d in range(NY)], axis=0)
            logits = logits + lax.dot_general(
                pg[m, k][:, :64], rows, (((1,), (0,)), ((), ())),
                preferred_element_type=jnp.float32,
            )
    rates = jnp.maximum(logits, 0.0) + jnp.log1p(jnp.exp(-jnp.abs(logits))) + rate_floor
    c_cnt.wait()
    observed = pltpu.roll(cnt_ref[...].astype(jnp.float32), shift, 1)[:, :128]
    observed = jnp.where(tile_lane < TR, observed, 0.0)
    part = [
        jnp.sum(rates, axis=0, keepdims=True),
        jnp.sum(observed, axis=0, keepdims=True),
        jnp.sum(observed * jnp.log(rates), axis=0, keepdims=True),
        jnp.zeros((5, 128), jnp.float32),
    ]
    ty[0, 0] = jnp.concatenate(part, axis=0)
    c_ty = [
        send(ty.at[0, 0], ty.at[a, b], s_ty.at[a, b], r_ty.at[a, b], both_dev(a, b))
        for a, b in group
    ]
    sig = 1.0 / (1.0 + jnp.exp(-logits))
    obs_rate = observed / rates
    for c in c_ty:
        c.wait_recv()
    tot = jnp.zeros((8, 128), jnp.float32)
    for a in range(NY):
        for b in range(NS):
            tot = tot + ty[(y + NY - a) % NY, (s + NS - b) % NS]
    pred = tot[0:1, :]
    obs = tot[1:2, :]
    log_pred = jnp.log(pred)
    lane = lax.broadcasted_iota(jnp.int32, (1, 128), 1)
    terms = total_weight * (pred - obs * log_pred) + obs * log_pred - tot[2:3, :]
    loss = jnp.sum(jnp.where(lane < TR, terms, 0.0), axis=1, keepdims=True)
    ratio = obs / pred
    grad_rates = total_weight * (1.0 - ratio) + ratio - obs_rate
    grad = grad_rates * sig
    hi = loss.astype(jnp.bfloat16).astype(jnp.float32)
    mid = (loss - hi).astype(jnp.bfloat16).astype(jnp.float32)
    lo = loss - hi - mid
    lanes = lax.broadcasted_iota(jnp.int32, (16, 128), 1)
    grad = jnp.where(
        lanes < TR, grad, jnp.where(lanes == TR, hi, jnp.where(lanes == TR + 1, mid, lo))
    )
    gg[0, 1, 0] = grad.astype(jnp.bfloat16)
    c_gf = [
        send(gg.at[0, 1, 0], gg.at[0, 1, e], s_gf.at[e], r_gf.at[e], zdev(-4 * FAR[e]))
        for e in range(7, 0, -1)
    ][::-1]
    c_gn = []
    c_gy = []

    def over_y(m, g):
        e, n = GROUPS[g]
        return [
            send(
                gg.at[0, m, e : e + n], gg.at[d, m, e : e + n], s_gy.at[d, m, g],
                r_gy.at[d, m, g], ydev(d),
            )
            for d in range(1, NY)
        ]

    for g in range(5):
        if g < 4:
            e, n = GROUPS[g]
            for c in c_gf[max(e, 1) - 1 : e + n - 1]:
                c.wait_recv()
            c_gn.append(
                [
                    send(
                        gg.at[0, 1, e : e + n], gg.at[0, m, e : e + n], s_gn.at[m, g],
                        r_gn.at[m, g], zdev(-o),
                    )
                    for m, o in near
                ]
            )
            c_gy += over_y(1, g)
        if g > 0:
            for c, (m, o) in zip(c_gn[g - 1], near):
                c.wait_recv()
                c_gy += over_y(m, g - 1)
    c_gn = [c for some in c_gn for c in some]

    by_z = jnp.zeros((1, 128), jnp.float32)
    for k in range(8):
        for m in range(4):
            row = gg[0, m, k][0:1, :].astype(jnp.float32)
            val = jnp.sum(
                jnp.where((lane >= TR) & (lane < TR + 3), row, 0.0), axis=1, keepdims=True
            )
            by_z = jnp.where(lane == (z + m - 1 + 4 * FAR[k] + NZ) % NZ, val, by_z)
    loss_ref[0, 0] = jnp.sum(by_z) * (1.0 / (512 * 3840))


    wl = jnp.concatenate([w_ref[FAR[k], m] for k in range(8) for m in range(4)], axis=1)

    def grad_block(d):
        gl = jnp.concatenate([gg[d, m, k] for k in range(8) for m in range(4)], axis=1)
        block = lax.dot_general(wl, gl, nt, preferred_element_type=jnp.float32)
        top, low = halves(block)
        for j in range(4):
            rows = lax.dot_general(top, spread[j], nn, preferred_element_type=jnp.float32)
            rows = rows + lax.dot_general(low, spread[j], nn, preferred_element_type=jnp.float32)
            oo[pl.ds((y + NY - d) % NY * 4 + j, 16, stride=16), :] = rows

    grad_block(0)
    for c in c_gy:
        c.wait_recv()
    for d in range(1, NY):
        grad_block(d)

    gated = oo[...] * query
    gg_out[...] = gated.astype(jnp.bfloat16).reshape(NS, 2, 16, 128)
    c_gx = [
        send(gg_out.at[(s + d) % NS], gx.at[d], s_gx.at[d], r_gx.at[d], sdev(d))
        for d in range(1, NS)
    ]
    gx[0] = gg_out[s]

    def give(p):
        for a in range(16):
            out_ref[p, :, 128 * a : 128 * a + 128] = mx[pl.ds(a, 16, stride=16), :]

    mx[...] = oo[...] * mx[...]
    give(0)
    for c in c_cv:
        c.wait_send()
    for c in c_gx:
        c.wait_recv()
    place(gx)

    def backward(c, carry):
        for d in range(16):
            sh[:, 128 * d : 128 * d + 128] = xp[c, 16 + d : 144 + d, :].astype(jnp.bfloat16)
        for p in range(4):
            taps = jnp.concatenate(
                [
                    jnp.concatenate([tt[c, 32 * p + 16 * h + e] for e in range(16)], axis=1)
                    for h in range(2)
                ],
                axis=0,
            )
            rows = 128 - 32 * p
            part = lax.dot_general(
                sh[32 * p : 128, :], taps, nt, preferred_element_type=jnp.float32
            )
            first = part[:, :128].reshape(8 - 2 * p, 16, 128)
            second = part[16:, 128:].reshape(7 - 2 * p, 16, 128)
            if p == 0:
                yy[c] = first
            else:
                yy[c, 0 : 8 - 2 * p] = yy[c, 0 : 8 - 2 * p] + first
            yy[c, 0 : 7 - 2 * p] = yy[c, 0 : 7 - 2 * p] + second
        return carry

    lax.fori_loop(0, 2, backward, 0)
    yb[...] = yy[...].astype(jnp.bfloat16)
    c_gr = [
        send(yb.at[:, (s + d) % NS], gr.at[d], s_gr.at[d], r_gr.at[d], sdev(d))
        for d in range(1, NS)
    ]
    gr[0] = yb[:, s]
    for c in c_gr:
        c.wait_recv()
    grad_kv = collect(gr) + skip * (oo[...] * query)
    mx[...] = grad_kv * x_ref[2]
    give(1)
    mx[...] = grad_kv * x_ref[1]
    give(2)

    for c in c_hx + c_kv + c_wa + c_py + c_wb + c_pf + c_pn + c_wy + c_ty:
        c.wait_send()
    for c in c_gf + c_gn + c_gy + c_gx + c_gr:
        c.wait_send()


def per_device(projections, filter_taps, skip_gain, head_weight, head_bias, counts):
    sem = pltpu.SemaphoreType.DMA
    b16 = jnp.bfloat16
    f32 = jnp.float32
    out, loss = pl.pallas_call(
        step_kernel,
        out_shape=(
            jax.ShapeDtypeStruct((3, 16, 2048), f32),
            jax.ShapeDtypeStruct((1, 1), f32),
        ),
        in_specs=[
            pl.BlockSpec(memory_space=space)
            for space in (pltpu.VMEM, pltpu.VMEM, pltpu.SMEM, pltpu.VMEM, pl.ANY, pltpu.VMEM)
        ],
        out_specs=(
            pl.BlockSpec(memory_space=pltpu.VMEM),
            pl.BlockSpec(memory_space=pltpu.SMEM),
        ),
        scratch_shapes=[
            pltpu.VMEM((3, 256, 128), f32),
            pltpu.VMEM((256, 128), f32),
            pltpu.VMEM((8, 2, 16, 128), b16),
            pltpu.VMEM((8, 4, 16, 128), b16),
            pltpu.VMEM((16, 256), jnp.int32),
            pltpu.VMEM((256, 128), f32),
            pltpu.VMEM((8, 2, 16, 128), b16),
            pltpu.VMEM((7, 2, 16, 128), b16),
            pltpu.VMEM((8, 2, 16, 128), b16),
            pltpu.VMEM((2, 160, 128), f32),
            pltpu.VMEM((2, 128, 128), f32),
            pltpu.VMEM((2, 1032, 128), f32),
            pltpu.VMEM((2, 1024, 256), b16),
            pltpu.VMEM((8, 256, 256), b16),
            pltpu.VMEM((128, 2048), b16),
            pltpu.VMEM((2, 128, 128, 128), b16),
            pltpu.VMEM((2, 8, 16, 128), f32),
            pltpu.VMEM((2, 8, 16, 128), b16),
            pltpu.VMEM((8, 2, 16, 128), b16),
            pltpu.VMEM((256, 128), f32),
            pltpu.VMEM((8, 2, 16, 128), b16),
            pltpu.VMEM((8, 2, 16, 128), b16),
            pltpu.VMEM((8, 2, 16, 128), b16),
            pltpu.VMEM((4, 16, 128), b16),
            pltpu.VMEM((4, 8, 16, 128), b16),
            pltpu.VMEM((4, 8, 4, 16, 128), b16),
            pltpu.VMEM((3, 16, 128), b16),
            pltpu.VMEM((4, 8, 16, 128), b16),
            pltpu.VMEM((4, 8, 8, 128), f32),
            pltpu.VMEM((4, 4, 8, 16, 128), b16),
            sem((3,)),
            sem((8,)), sem((8,)), sem((8,)), sem((8,)), sem((8,)), sem((8,)),
            sem((8,)), sem((8,)), sem((8,)), sem((8,)),
            sem((4,)), sem((4,)), sem((8,)), sem((8,)), sem((4, 4)), sem((4, 4)),
            sem((4,)), sem((4,)), sem((8,)), sem((8,)), sem((4, 4)), sem((4, 4)),
            sem((4, 8)), sem((4, 8)), sem((8,)), sem((8,)),
            sem((4, 4)), sem((4, 4)), sem((4, 4, 4)), sem((4, 4, 4)),
        ],
        compiler_params=pltpu.CompilerParams(collective_id=0, has_side_effects=True),
    )(projections, filter_taps, skip_gain, head_weight, counts, head_bias.reshape(1, -1))
    return loss.reshape(()), out


def solution(mesh):
    placed = (
        P(None, "chan", "seq"),
        P("chan", "seq"),
        P("chan"),
        P("chan", None),
        P(),
        P("seq", None),
    )
    return jax.shard_map(
        per_device,
        mesh=mesh,
        in_specs=placed,
        out_specs=(P(), P(None, "chan", "seq")),
        check_vma=False,
    )
```

```python
import jax
import jax.numpy as jnp
from jax import lax
from jax.experimental import pallas as pl
from jax.experimental.pallas import tpu as pltpu
from jax.sharding import PartitionSpec as P

POOL = 32
NY = 4
NZ = 32
NS = 8
TR = 120
FAR = (0, 1, 7, 2, 6, 3, 5, 4)
GROUPS = ((0, 3), (3, 2), (5, 2), (7, 1))
MESH = pl.DeviceIdType.MESH

total_weight = 0.2
rate_floor = 0.5


def step_kernel(
    proj_ref, taps_ref, skip_ref, head_ref, count_ref, bias_ref,
    out_ref, loss_ref,
    x_ref, ht, h_ref, w_ref, cnt_ref, mx, kv, hx, rx, xp, hf, vf, vb, pick, sh, tt, yy, yb, cv, oo, gx, gg_out, gr, pp,
    wa, wg, py, pg, ty, gg,
    entered, s_loc, s_kv, r_kv, s_hx, r_hx, s_cv, r_cv, s_gx, r_gx, s_gr, r_gr,
    s_wa, r_wa, s_wb, r_wb, s_wy, r_wy, s_py, r_py, s_pf, r_pf, s_pn, r_pn,
    s_ty, r_ty, s_gf, r_gf, s_gn, r_gn, s_gy, r_gy,
):
    s = lax.axis_index("seq")
    ch = lax.axis_index("chan")
    y = ch // NZ
    z = ch % NZ

    def zdev(d):
        return (s, y * NZ + (z + d + NZ) % NZ)

    def ydev(d):
        return (s, ((y + d) % NY) * NZ + z)

    def sdev(d):
        return ((s + d) % NS, ch)

    def both_dev(a, b):
        return ((s + b) % NS, ((y + a) % NY) * NZ + z)

    def send(src, dst, ss, rs, dev):
        c = pltpu.make_async_remote_copy(
            src_ref=src, dst_ref=dst, send_sem=ss, recv_sem=rs, device_id=dev, device_id_type=MESH
        )
        c.start()
        return c

    near = ((0, -1), (2, 1), (3, 2))

    barrier = pltpu.get_barrier_semaphore()
    group = [(a, b) for a in range(NY) for b in range(NS) if a or b]
    peers = [sdev(d) for d in range(1, NS)] + [ydev(d) for d in range(1, NY)]
    peers += [zdev(d) for d in (-2, -1, 1, 2)]
    for dev in peers:
        pl.semaphore_signal(barrier, inc=1, device_id=dev, device_id_type=MESH)


    base = 120 * z // 128 - z // 31
    shift = (256 - (120 * z - 128 * base)) % 256
    base = pl.multiple_of(128 * base, 128)
    c_cnt = pltpu.make_async_copy(
        count_ref.at[pl.ds(pl.multiple_of(16 * y, 16), 16), pl.ds(base, 256)], cnt_ref, s_loc.at[2]
    )
    c_cnt.start()
    for a in range(16):
        for p in range(3):
            x_ref[p, pl.ds(a, 16, stride=16), :] = proj_ref[
                p, :, 128 * a : 128 * a + 128
            ].astype(jnp.float32)
        ht[pl.ds(a, 16, stride=16), :] = taps_ref[:, 128 * a : 128 * a + 128]
    h_ref[...] = ht[...].astype(jnp.bfloat16).reshape(NS, 2, 16, 128)
    tile_lane = lax.broadcasted_iota(jnp.int32, (16, 128), 1)
    for t in range(NZ):
        first = min(TR * t // 128, 28) * 128
        tile = head_ref[:, first : first + 256].astype(jnp.float32)
        tile = pltpu.roll(tile, (256 - (TR * t - first)) % 256, 1)[:, :128]
        at = (t + NZ + 1 - z) % NZ
        w_ref[at // 4, at % 4] = jnp.where(tile_lane < TR, tile, 0.0).astype(jnp.bfloat16)
    key_value = x_ref[1] * x_ref[2]
    kv[...] = key_value.astype(jnp.bfloat16).reshape(NS, 2, 16, 128)
    for c in range(2):
        xp[c, 0:16, :] = jnp.zeros((16, 128), jnp.float32)
        xp[c, 144:160, :] = jnp.zeros((16, 128), jnp.float32)
        vf[c, 0:8, :] = jnp.zeros((8, 128), jnp.float32)
    tall = lax.broadcasted_iota(jnp.int32, (256, 256), 0)
    wide = lax.broadcasted_iota(jnp.int32, (256, 256), 1)
    for q in range(8):
        pick[q] = jnp.where(
            tall == 128 + wide % 128 - 16 * q - 8 * (wide // 128), 1.0, 0.0
        ).astype(jnp.bfloat16)
    pl.semaphore_wait(barrier, len(peers))

    def tell(step):
        for side in range(2):
            pl.semaphore_signal(
                entered.at[step, side], inc=1, device_id=zdev((2 - 4 * side) * 2**step),
                device_id_type=MESH,
            )

    def hear(step):
        for side in range(2):
            pl.semaphore_wait(entered.at[step, side], 1)

    tell(0)
    c_hx = [
        send(h_ref.at[(s + d) % NS], hx.at[d - 1], s_hx.at[d], r_hx.at[d], sdev(d))
        for d in range(1, NS)
    ]
    c_kv = [
        send(kv.at[(s + d) % NS], rx.at[d], s_kv.at[d], r_kv.at[d], sdev(d)) for d in range(1, NS)
    ]
    c_wa = [send(w_ref.at[:, m], wa.at[m], s_wa.at[m], r_wa.at[m], zdev(o)) for m, o in near]
    own_wa = pltpu.make_async_copy(w_ref.at[:, 1], wa.at[1], s_loc.at[0])
    own_wa.start()
    for c in c_hx:
        c.wait_recv()

    def put_taps(d, block):
        a = pl.multiple_of((s + NS - d) % NS * 16, 16)
        for c in range(2):
            hf[c, pl.ds(a, 16), :] = block[c].astype(jnp.float32)

    put_taps(0, h_ref[s])
    for d in range(1, NS):
        put_taps(d, hx[d - 1])
    hear(0)
    tell(1)

    lane8 = lax.broadcasted_iota(jnp.int32, (8, 128), 1)
    sub8 = lax.broadcasted_iota(jnp.int32, (8, 128), 0)

    def windows(c):
        def body(d, last):
            line = jnp.broadcast_to(hf[c, pl.ds(d, 1), :], (8, 128))
            now = pltpu.roll(line, 0, 1, stride=1, stride_axis=0)
            vf[c, pl.ds(pl.multiple_of(8 + 8 * d, 8), 8), :] = jnp.where(
                lane8 >= sub8, now, last
            )
            return now

        lax.fori_loop(0, 128, body, jnp.zeros((8, 128), jnp.float32), unroll=16)
        vb[c, :, 0:128] = vf[c, 0:1024, :].astype(jnp.bfloat16)
        vb[c, :, 128:256] = vf[c, 8:1032, :].astype(jnp.bfloat16)

    windows(0)
    windows(1)
    hear(1)
    tell(2)

    def fill(q, carry):
        for c in range(2):
            block = jnp.dot(vb[c], pick[q], preferred_element_type=jnp.float32)
            both = jnp.concatenate(
                [block[:, :128].reshape(128, 8, 128), block[:, 128:].reshape(128, 8, 128)], axis=1
            )
            tt[c, :, pl.ds(pl.multiple_of(16 * q, 16), 16), :] = both.astype(jnp.bfloat16)
        return carry

    lax.fori_loop(0, 8, fill, 0)

    def place(blocks):
        for a in range(NS):
            for c in range(2):
                xp[c, 16 + 16 * a : 32 + 16 * a, :] = blocks[(s + NS - a) % NS, c].astype(
                    jnp.float32
                )

    for c in c_kv:
        c.wait_recv()
    rx[0] = kv[s]
    place(rx)

    def forward(c, carry):
        for d in range(16):
            sh[:, 128 * d : 128 * d + 128] = xp[c, 16 - d : 144 - d, :].astype(jnp.bfloat16)
        for p in range(4):
            taps = jnp.concatenate(
                [tt[c, 32 * p + 16 * h : 32 * p + 16 * h + 16].reshape(2048, 128) for h in range(2)],
                axis=1,
            )
            rows = 128 - 32 * p
            part = jnp.dot(sh[0:rows, :], taps, preferred_element_type=jnp.float32)
            first = part[:, :128].reshape(8 - 2 * p, 16, 128)
            second = part[: rows - 16, 128:].reshape(7 - 2 * p, 16, 128)
            if p == 0:
                yy[c] = first
            else:
                yy[c, 2 * p : 8] = yy[c, 2 * p : 8] + first
            yy[c, 2 * p + 1 : 8] = yy[c, 2 * p + 1 : 8] + second
        return carry

    lax.fori_loop(0, 2, forward, 0)
    yb[...] = yy[...].astype(jnp.bfloat16)
    c_cv = [
        send(yb.at[:, (s + d) % NS], cv.at[d], s_cv.at[d], r_cv.at[d], sdev(d))
        for d in range(1, NS)
    ]
    cv[0] = yb[:, s]
    hear(2)
    own_wa.wait()
    for c in c_wa:
        c.wait_recv()
    c_wb = [
        send(wa.at[:, FAR[e]], wg.at[0, e], s_wb.at[e], r_wb.at[e], zdev(4 * FAR[e]))
        for e in range(7, 0, -1)
    ][::-1]
    own_wb = pltpu.make_async_copy(wa.at[:, 0], wg.at[0, 0], s_loc.at[1])
    own_wb.start()
    for c in c_cv:
        c.wait_recv()

    def collect(blocks):
        return jnp.concatenate(
            [blocks[(s + NS - a) % NS].astype(jnp.float32).reshape(32, 128) for a in range(NS)], axis=0
        )

    skip = jnp.concatenate(
        [jnp.full((16, 128), skip_ref[c], jnp.float32) for c in range(16)], axis=0
    )
    query = x_ref[0]
    mixed = collect(cv) + skip * key_value
    oo[...] = query * mixed
    mx[...] = mixed

    small_row = lax.broadcasted_iota(jnp.int32, (16, 128), 0)
    small_col = lax.broadcasted_iota(jnp.int32, (16, 128), 1)
    spread = [
        jnp.where(
            (small_row // 4 == j) & (small_col // 32 == small_row % 4), 1.0 / POOL, 0.0
        ).astype(jnp.bfloat16)
        for j in range(4)
    ]

    def halves(val):
        top = val.astype(jnp.bfloat16)
        return top, (val - top.astype(jnp.float32)).astype(jnp.bfloat16)

    nt = (((1,), (1,)), ((), ()))
    nn = (((1,), (0,)), ((), ()))
    for d in range(NY):
        mean = jnp.zeros((16, 16), jnp.float32)
        for j in range(4):
            rows = oo[pl.ds((y + d) % NY * 4 + j, 16, stride=16), :]
            for piece in halves(rows):
                mean = mean + lax.dot_general(
                    spread[j], piece, nt, preferred_element_type=jnp.float32
                )
        lanes_of = (small_col == small_row + 16 * d).astype(jnp.float32).astype(jnp.bfloat16)
        pp[d] = lax.dot_general(
            mean.astype(jnp.bfloat16), lanes_of, nn, preferred_element_type=jnp.float32
        ).astype(jnp.bfloat16)
    c_py = [
        send(pp.at[d], py.at[d - 1], s_py.at[d], r_py.at[d], ydev(d)) for d in range(1, NY)
    ]
    for c in c_py:
        c.wait_recv()
    tile = pp[0].astype(jnp.float32)
    for d in range(NY - 1):
        tile = tile + py[d].astype(jnp.float32)
    pg[1, 0] = tile.astype(jnp.bfloat16)
    c_pf = [
        send(pg.at[1, 0], pg.at[1, e], s_pf.at[e], r_pf.at[e], zdev(4 * FAR[e]))
        for e in range(7, 0, -1)
    ][::-1]
    own_wb.wait()
    c_pn = []
    c_wy = []
    for g, (e, n) in enumerate(GROUPS):
        for c in c_pf[max(e, 1) - 1 : e + n - 1]:
            c.wait_recv()
        c_pn += [
            send(pg.at[1, e : e + n], pg.at[m, e : e + n], s_pn.at[m, g], r_pn.at[m, g], zdev(o))
            for m, o in near
        ]
        for c in c_wb[max(e, 1) - 1 : e + n - 1]:
            c.wait_recv()
        c_wy += [
            send(wg.at[0, e : e + n], wg.at[d, e : e + n], s_wy.at[d, g], r_wy.at[d, g], ydev(d))
            for d in range(1, NY)
        ]
    for c in c_pn:
        c.wait_recv()
    for c in c_wy:
        c.wait_recv()

    line = base // 128
    bias = jnp.concatenate([bias_ref[pl.ds(line + a, 1), :] for a in range(2)], axis=1)
    bias = jnp.broadcast_to(bias, (16, 256))
    bias = pltpu.roll(bias, shift, 1)[:, :128]
    logits = jnp.where(tile_lane < TR, bias, 0.0)
    for k in range(8):
        for m in range(4):
            rows = jnp.concatenate([wg[d, k, m] for d in range(NY)], axis=0)
            logits = logits + lax.dot_general(
                pg[m, k][:, :64], rows, (((1,), (0,)), ((), ())),
                preferred_element_type=jnp.float32,
            )
    rates = jnp.maximum(logits, 0.0) + jnp.log1p(jnp.exp(-jnp.abs(logits))) + rate_floor
    c_cnt.wait()
    observed = pltpu.roll(cnt_ref[...].astype(jnp.float32), shift, 1)[:, :128]
    observed = jnp.where(tile_lane < TR, observed, 0.0)
    part = [
        jnp.sum(rates, axis=0, keepdims=True),
        jnp.sum(observed, axis=0, keepdims=True),
        jnp.sum(observed * jnp.log(rates), axis=0, keepdims=True),
        jnp.zeros((5, 128), jnp.float32),
    ]
    ty[0, 0] = jnp.concatenate(part, axis=0)
    c_ty = [
        send(ty.at[0, 0], ty.at[a, b], s_ty.at[a, b], r_ty.at[a, b], both_dev(a, b))
        for a, b in group
    ]
    sig = 1.0 / (1.0 + jnp.exp(-logits))
    obs_rate = observed / rates
    for c in c_ty:
        c.wait_recv()
    tot = jnp.zeros((8, 128), jnp.float32)
    for a in range(NY):
        for b in range(NS):
            tot = tot + ty[(y + NY - a) % NY, (s + NS - b) % NS]
    pred = tot[0:1, :]
    obs = tot[1:2, :]
    log_pred = jnp.log(pred)
    lane = lax.broadcasted_iota(jnp.int32, (1, 128), 1)
    terms = total_weight * (pred - obs * log_pred) + obs * log_pred - tot[2:3, :]
    loss = jnp.sum(jnp.where(lane < TR, terms, 0.0), axis=1, keepdims=True)
    ratio = obs / pred
    grad_rates = total_weight * (1.0 - ratio) + ratio - obs_rate
    grad = grad_rates * sig
    hi = loss.astype(jnp.bfloat16).astype(jnp.float32)
    mid = (loss - hi).astype(jnp.bfloat16).astype(jnp.float32)
    lo = loss - hi - mid
    lanes = lax.broadcasted_iota(jnp.int32, (16, 128), 1)
    grad = jnp.where(
        lanes < TR, grad, jnp.where(lanes == TR, hi, jnp.where(lanes == TR + 1, mid, lo))
    )
    gg[0, 1, 0] = grad.astype(jnp.bfloat16)
    c_gf = [
        send(gg.at[0, 1, 0], gg.at[0, 1, e], s_gf.at[e], r_gf.at[e], zdev(-4 * FAR[e]))
        for e in range(7, 0, -1)
    ][::-1]
    c_gn = []
    c_gy = []

    def over_y(m, g):
        e, n = GROUPS[g]
        return [
            send(
                gg.at[0, m, e : e + n], gg.at[d, m, e : e + n], s_gy.at[d, m, g],
                r_gy.at[d, m, g], ydev(d),
            )
            for d in range(1, NY)
        ]

    for g in range(5):
        if g < 4:
            e, n = GROUPS[g]
            for c in c_gf[max(e, 1) - 1 : e + n - 1]:
                c.wait_recv()
            c_gn.append(
                [
                    send(
                        gg.at[0, 1, e : e + n], gg.at[0, m, e : e + n], s_gn.at[m, g],
                        r_gn.at[m, g], zdev(-o),
                    )
                    for m, o in near
                ]
            )
            c_gy += over_y(1, g)
        if g > 0:
            for c, (m, o) in zip(c_gn[g - 1], near):
                c.wait_recv()
                c_gy += over_y(m, g - 1)
    c_gn = [c for some in c_gn for c in some]

    by_z = jnp.zeros((1, 128), jnp.float32)
    for k in range(8):
        for m in range(4):
            row = gg[0, m, k][0:1, :].astype(jnp.float32)
            val = jnp.sum(
                jnp.where((lane >= TR) & (lane < TR + 3), row, 0.0), axis=1, keepdims=True
            )
            by_z = jnp.where(lane == (z + m - 1 + 4 * FAR[k] + NZ) % NZ, val, by_z)
    loss_ref[0, 0] = jnp.sum(by_z) * (1.0 / (512 * 3840))


    wl = jnp.concatenate([w_ref[FAR[k], m] for k in range(8) for m in range(4)], axis=1)

    def grad_block(d):
        gl = jnp.concatenate([gg[d, m, k] for k in range(8) for m in range(4)], axis=1)
        block = lax.dot_general(wl, gl, nt, preferred_element_type=jnp.float32)
        top, low = halves(block)
        for j in range(4):
            rows = lax.dot_general(top, spread[j], nn, preferred_element_type=jnp.float32)
            rows = rows + lax.dot_general(low, spread[j], nn, preferred_element_type=jnp.float32)
            oo[pl.ds((y + NY - d) % NY * 4 + j, 16, stride=16), :] = rows

    grad_block(0)
    for c in c_gy:
        c.wait_recv()
    for d in range(1, NY):
        grad_block(d)

    gated = oo[...] * query
    gg_out[...] = gated.astype(jnp.bfloat16).reshape(NS, 2, 16, 128)
    c_gx = [
        send(gg_out.at[(s + d) % NS], gx.at[d], s_gx.at[d], r_gx.at[d], sdev(d))
        for d in range(1, NS)
    ]
    gx[0] = gg_out[s]

    def give(p):
        for a in range(16):
            out_ref[p, :, 128 * a : 128 * a + 128] = mx[pl.ds(a, 16, stride=16), :]

    mx[...] = oo[...] * mx[...]
    give(0)
    for c in c_cv:
        c.wait_send()
    for c in c_gx:
        c.wait_recv()
    place(gx)

    def backward(c, carry):
        for d in range(16):
            sh[:, 128 * d : 128 * d + 128] = xp[c, 16 + d : 144 + d, :].astype(jnp.bfloat16)
        for p in range(4):
            taps = jnp.concatenate(
                [
                    jnp.concatenate([tt[c, 32 * p + 16 * h + e] for e in range(16)], axis=1)
                    for h in range(2)
                ],
                axis=0,
            )
            rows = 128 - 32 * p
            part = lax.dot_general(
                sh[32 * p : 128, :], taps, nt, preferred_element_type=jnp.float32
            )
            first = part[:, :128].reshape(8 - 2 * p, 16, 128)
            second = part[16:, 128:].reshape(7 - 2 * p, 16, 128)
            if p == 0:
                yy[c] = first
            else:
                yy[c, 0 : 8 - 2 * p] = yy[c, 0 : 8 - 2 * p] + first
            yy[c, 0 : 7 - 2 * p] = yy[c, 0 : 7 - 2 * p] + second
        return carry

    lax.fori_loop(0, 2, backward, 0)
    yb[...] = yy[...].astype(jnp.bfloat16)
    c_gr = [
        send(yb.at[:, (s + d) % NS], gr.at[d], s_gr.at[d], r_gr.at[d], sdev(d))
        for d in range(1, NS)
    ]
    gr[0] = yb[:, s]
    for c in c_gr:
        c.wait_recv()
    grad_kv = collect(gr) + skip * (oo[...] * query)
    mx[...] = grad_kv * x_ref[2]
    give(1)
    mx[...] = grad_kv * x_ref[1]
    give(2)

    for c in c_hx + c_kv + c_wa + c_py + c_wb + c_pf + c_pn + c_wy + c_ty:
        c.wait_send()
    for c in c_gf + c_gn + c_gy + c_gx + c_gr:
        c.wait_send()


def per_device(projections, filter_taps, skip_gain, head_weight, head_bias, counts):
    sem = pltpu.SemaphoreType.DMA
    b16 = jnp.bfloat16
    f32 = jnp.float32
    out, loss = pl.pallas_call(
        step_kernel,
        out_shape=(
            jax.ShapeDtypeStruct((3, 16, 2048), f32),
            jax.ShapeDtypeStruct((1, 1), f32),
        ),
        in_specs=[
            pl.BlockSpec(memory_space=space)
            for space in (pltpu.VMEM, pltpu.VMEM, pltpu.SMEM, pltpu.VMEM, pl.ANY, pltpu.VMEM)
        ],
        out_specs=(
            pl.BlockSpec(memory_space=pltpu.VMEM),
            pl.BlockSpec(memory_space=pltpu.SMEM),
        ),
        scratch_shapes=[
            pltpu.VMEM((3, 256, 128), f32),
            pltpu.VMEM((256, 128), f32),
            pltpu.VMEM((8, 2, 16, 128), b16),
            pltpu.VMEM((8, 4, 16, 128), b16),
            pltpu.VMEM((16, 256), jnp.int32),
            pltpu.VMEM((256, 128), f32),
            pltpu.VMEM((8, 2, 16, 128), b16),
            pltpu.VMEM((7, 2, 16, 128), b16),
            pltpu.VMEM((8, 2, 16, 128), b16),
            pltpu.VMEM((2, 160, 128), f32),
            pltpu.VMEM((2, 128, 128), f32),
            pltpu.VMEM((2, 1032, 128), f32),
            pltpu.VMEM((2, 1024, 256), b16),
            pltpu.VMEM((8, 256, 256), b16),
            pltpu.VMEM((128, 2048), b16),
            pltpu.VMEM((2, 128, 128, 128), b16),
            pltpu.VMEM((2, 8, 16, 128), f32),
            pltpu.VMEM((2, 8, 16, 128), b16),
            pltpu.VMEM((8, 2, 16, 128), b16),
            pltpu.VMEM((256, 128), f32),
            pltpu.VMEM((8, 2, 16, 128), b16),
            pltpu.VMEM((8, 2, 16, 128), b16),
            pltpu.VMEM((8, 2, 16, 128), b16),
            pltpu.VMEM((4, 16, 128), b16),
            pltpu.VMEM((4, 8, 16, 128), b16),
            pltpu.VMEM((4, 8, 4, 16, 128), b16),
            pltpu.VMEM((3, 16, 128), b16),
            pltpu.VMEM((4, 8, 16, 128), b16),
            pltpu.VMEM((4, 8, 8, 128), f32),
            pltpu.VMEM((4, 4, 8, 16, 128), b16),
            pltpu.SemaphoreType.REGULAR((3, 2)),
            sem((3,)),
            sem((8,)), sem((8,)), sem((8,)), sem((8,)), sem((8,)), sem((8,)),
            sem((8,)), sem((8,)), sem((8,)), sem((8,)),
            sem((4,)), sem((4,)), sem((8,)), sem((8,)), sem((4, 4)), sem((4, 4)),
            sem((4,)), sem((4,)), sem((8,)), sem((8,)), sem((4, 4)), sem((4, 4)),
            sem((4, 8)), sem((4, 8)), sem((8,)), sem((8,)),
            sem((4, 4)), sem((4, 4)), sem((4, 4, 4)), sem((4, 4, 4)),
        ],
        compiler_params=pltpu.CompilerParams(collective_id=0, has_side_effects=True),
    )(projections, filter_taps, skip_gain, head_weight, counts, head_bias.reshape(-1, 128))
    return loss.reshape(()), out


def solution(mesh):
    placed = (
        P(None, "chan", "seq"),
        P("chan", "seq"),
        P("chan"),
        P("chan", None),
        P(),
        P("seq", None),
    )
    return jax.shard_map(
        per_device,
        mesh=mesh,
        in_specs=placed,
        out_specs=(P(), P(None, "chan", "seq")),
        check_vma=False,
    )
```

```python
import jax
import jax.numpy as jnp
from jax import lax
from jax.experimental import pallas as pl
from jax.experimental.pallas import tpu as pltpu
from jax.sharding import PartitionSpec as P

POOL = 32
NY = 4
NZ = 32
NS = 8
TR = 120
FAR = (0, 1, 7, 2, 6, 3, 5, 4)
GROUPS = ((0, 3), (3, 2), (5, 2), (7, 1))
MESH = pl.DeviceIdType.MESH

total_weight = 0.2
rate_floor = 0.5


def step_kernel(
    proj_ref, taps_ref, skip_ref, head_ref, count_ref, bias_ref,
    out_ref, loss_ref,
    x_ref, ht, h_ref, w_ref, cnt_ref, mx, kv, hx, rx, xp, hf, vf, vb, pick, sh, tt, yy, yb, cv, oo, gx, gg_out, gr, pp,
    wa, wg, py, pg, ty, gg,
    entered, s_loc, s_kv, r_kv, s_hx, r_hx, s_cv, r_cv, s_gx, r_gx, s_gr, r_gr,
    s_wa, r_wa, s_wb, r_wb, s_wy, r_wy, s_py, r_py, s_pf, r_pf, s_pn, r_pn,
    s_ty, r_ty, s_gf, r_gf, s_gn, r_gn, s_gy, r_gy,
):
    s = lax.axis_index("seq")
    ch = lax.axis_index("chan")
    y = ch // NZ
    z = ch % NZ

    def zdev(d):
        return (s, y * NZ + (z + d + NZ) % NZ)

    def ydev(d):
        return (s, ((y + d) % NY) * NZ + z)

    def sdev(d):
        return ((s + d) % NS, ch)

    def both_dev(a, b):
        return ((s + b) % NS, ((y + a) % NY) * NZ + z)

    def send(src, dst, ss, rs, dev):
        c = pltpu.make_async_remote_copy(
            src_ref=src, dst_ref=dst, send_sem=ss, recv_sem=rs, device_id=dev, device_id_type=MESH
        )
        c.start()
        return c

    near = ((0, -1), (2, 1), (3, 2))

    barrier = pltpu.get_barrier_semaphore()
    group = [(a, b) for a in range(NY) for b in range(NS) if a or b]
    peers = [sdev(d) for d in range(1, NS)] + [ydev(d) for d in range(1, NY)]
    peers += [zdev(d) for d in (-2, -1, 1, 2)]
    for dev in peers:
        pl.semaphore_signal(barrier, inc=1, device_id=dev, device_id_type=MESH)


    base = 120 * z // 128 - z // 31
    shift = (256 - (120 * z - 128 * base)) % 256
    base = pl.multiple_of(128 * base, 128)
    c_cnt = pltpu.make_async_copy(
        count_ref.at[pl.ds(pl.multiple_of(16 * y, 16), 16), pl.ds(base, 256)], cnt_ref, s_loc.at[2]
    )
    c_cnt.start()
    for a in range(16):
        for p in range(3):
            x_ref[p, pl.ds(a, 16, stride=16), :] = proj_ref[
                p, :, 128 * a : 128 * a + 128
            ].astype(jnp.float32)
        ht[pl.ds(a, 16, stride=16), :] = taps_ref[:, 128 * a : 128 * a + 128]
    h_ref[...] = ht[...].astype(jnp.bfloat16).reshape(NS, 2, 16, 128)
    tile_lane = lax.broadcasted_iota(jnp.int32, (16, 128), 1)
    for t in range(NZ):
        first = min(TR * t // 128, 28) * 128
        tile = head_ref[:, first : first + 256].astype(jnp.float32)
        tile = pltpu.roll(tile, (256 - (TR * t - first)) % 256, 1)[:, :128]
        at = (t + NZ + 1 - z) % NZ
        w_ref[at // 4, at % 4] = jnp.where(tile_lane < TR, tile, 0.0).astype(jnp.bfloat16)
    key_value = x_ref[1] * x_ref[2]
    kv[...] = key_value.astype(jnp.bfloat16).reshape(NS, 2, 16, 128)
    for c in range(2):
        xp[c, 0:16, :] = jnp.zeros((16, 128), jnp.float32)
        xp[c, 144:160, :] = jnp.zeros((16, 128), jnp.float32)
        vf[c, 0:8, :] = jnp.zeros((8, 128), jnp.float32)
    tall = lax.broadcasted_iota(jnp.int32, (256, 256), 0)
    wide = lax.broadcasted_iota(jnp.int32, (256, 256), 1)
    for q in range(8):
        pick[q] = jnp.where(
            tall == 128 + wide % 128 - 16 * q - 8 * (wide // 128), 1.0, 0.0
        ).astype(jnp.bfloat16)
    pl.semaphore_wait(barrier, len(peers))

    def tell(step):
        for side in range(2):
            pl.semaphore_signal(
                entered.at[step, side], inc=1, device_id=zdev((2 - 4 * side) * 2**step),
                device_id_type=MESH,
            )

    def hear(step):
        for side in range(2):
            pl.semaphore_wait(entered.at[step, side], 1)

    tell(0)
    c_hx = [
        send(h_ref.at[(s + d) % NS], hx.at[d - 1], s_hx.at[d], r_hx.at[d], sdev(d))
        for d in range(1, NS)
    ]
    c_kv = [
        send(kv.at[(s + d) % NS], rx.at[d], s_kv.at[d], r_kv.at[d], sdev(d)) for d in range(1, NS)
    ]
    c_wa = [send(w_ref.at[:, m], wa.at[m], s_wa.at[m], r_wa.at[m], zdev(o)) for m, o in near]
    own_wa = pltpu.make_async_copy(w_ref.at[:, 1], wa.at[1], s_loc.at[0])
    own_wa.start()
    for c in c_hx:
        c.wait_recv()

    def put_taps(d, block):
        a = pl.multiple_of((s + NS - d) % NS * 16, 16)
        for c in range(2):
            hf[c, pl.ds(a, 16), :] = block[c].astype(jnp.float32)

    put_taps(0, h_ref[s])
    for d in range(1, NS):
        put_taps(d, hx[d - 1])
    hear(0)
    tell(1)

    lane8 = lax.broadcasted_iota(jnp.int32, (8, 128), 1)
    sub8 = lax.broadcasted_iota(jnp.int32, (8, 128), 0)

    def windows(c):
        def body(d, last):
            line = jnp.broadcast_to(hf[c, pl.ds(d, 1), :], (8, 128))
            now = pltpu.roll(line, 0, 1, stride=1, stride_axis=0)
            vf[c, pl.ds(pl.multiple_of(8 + 8 * d, 8), 8), :] = jnp.where(
                lane8 >= sub8, now, last
            )
            return now

        lax.fori_loop(0, 128, body, jnp.zeros((8, 128), jnp.float32), unroll=16)
        vb[c, :, 0:128] = vf[c, 0:1024, :].astype(jnp.bfloat16)
        vb[c, :, 128:256] = vf[c, 8:1032, :].astype(jnp.bfloat16)

    windows(0)
    windows(1)
    hear(1)
    tell(2)

    def fill(q, carry):
        for c in range(2):
            block = jnp.dot(vb[c], pick[q], preferred_element_type=jnp.float32)
            both = jnp.concatenate(
                [block[:, :128].reshape(128, 8, 128), block[:, 128:].reshape(128, 8, 128)], axis=1
            )
            tt[c, :, pl.ds(pl.multiple_of(16 * q, 16), 16), :] = both.astype(jnp.bfloat16)
        return carry

    lax.fori_loop(0, 8, fill, 0, unroll=4)

    def place(blocks):
        for a in range(NS):
            for c in range(2):
                xp[c, 16 + 16 * a : 32 + 16 * a, :] = blocks[(s + NS - a) % NS, c].astype(
                    jnp.float32
                )

    for c in c_kv:
        c.wait_recv()
    rx[0] = kv[s]
    place(rx)

    def forward(c, carry):
        for d in range(16):
            sh[c, :, 128 * d : 128 * d + 128] = xp[c, 16 - d : 144 - d, :].astype(jnp.bfloat16)
        for p in range(4):
            taps = jnp.concatenate(
                [tt[c, 32 * p + 16 * h : 32 * p + 16 * h + 16].reshape(2048, 128) for h in range(2)],
                axis=1,
            )
            rows = 128 - 32 * p
            part = jnp.dot(sh[c, 0:rows, :], taps, preferred_element_type=jnp.float32)
            first = part[:, :128].reshape(8 - 2 * p, 16, 128)
            second = part[: rows - 16, 128:].reshape(7 - 2 * p, 16, 128)
            if p == 0:
                yy[c] = first
            else:
                yy[c, 2 * p : 8] = yy[c, 2 * p : 8] + first
            yy[c, 2 * p + 1 : 8] = yy[c, 2 * p + 1 : 8] + second
        return carry

    for c in range(2):
        forward(c, 0)
    yb[...] = yy[...].astype(jnp.bfloat16)
    c_cv = [
        send(yb.at[:, (s + d) % NS], cv.at[d], s_cv.at[d], r_cv.at[d], sdev(d))
        for d in range(1, NS)
    ]
    cv[0] = yb[:, s]
    hear(2)
    own_wa.wait()
    for c in c_wa:
        c.wait_recv()
    c_wb = [
        send(wa.at[:, FAR[e]], wg.at[0, e], s_wb.at[e], r_wb.at[e], zdev(4 * FAR[e]))
        for e in range(7, 0, -1)
    ][::-1]
    own_wb = pltpu.make_async_copy(wa.at[:, 0], wg.at[0, 0], s_loc.at[1])
    own_wb.start()
    for c in c_cv:
        c.wait_recv()

    def collect(blocks):
        return jnp.concatenate(
            [blocks[(s + NS - a) % NS].astype(jnp.float32).reshape(32, 128) for a in range(NS)], axis=0
        )

    skip = jnp.concatenate(
        [jnp.full((16, 128), skip_ref[c], jnp.float32) for c in range(16)], axis=0
    )
    query = x_ref[0]
    mixed = collect(cv) + skip * key_value
    oo[...] = query * mixed
    mx[...] = mixed

    small_row = lax.broadcasted_iota(jnp.int32, (16, 128), 0)
    small_col = lax.broadcasted_iota(jnp.int32, (16, 128), 1)
    spread = [
        jnp.where(
            (small_row // 4 == j) & (small_col // 32 == small_row % 4), 1.0 / POOL, 0.0
        ).astype(jnp.bfloat16)
        for j in range(4)
    ]

    def halves(val):
        top = val.astype(jnp.bfloat16)
        return top, (val - top.astype(jnp.float32)).astype(jnp.bfloat16)

    nt = (((1,), (1,)), ((), ()))
    nn = (((1,), (0,)), ((), ()))
    for d in range(NY):
        mean = jnp.zeros((16, 16), jnp.float32)
        for j in range(4):
            rows = oo[pl.ds((y + d) % NY * 4 + j, 16, stride=16), :]
            for piece in halves(rows):
                mean = mean + lax.dot_general(
                    spread[j], piece, nt, preferred_element_type=jnp.float32
                )
        lanes_of = (small_col == small_row + 16 * d).astype(jnp.float32).astype(jnp.bfloat16)
        pp[d] = lax.dot_general(
            mean.astype(jnp.bfloat16), lanes_of, nn, preferred_element_type=jnp.float32
        ).astype(jnp.bfloat16)
    c_py = [
        send(pp.at[d], py.at[d - 1], s_py.at[d], r_py.at[d], ydev(d)) for d in range(1, NY)
    ]
    for c in c_py:
        c.wait_recv()
    tile = pp[0].astype(jnp.float32)
    for d in range(NY - 1):
        tile = tile + py[d].astype(jnp.float32)
    pg[1, 0] = tile.astype(jnp.bfloat16)
    c_pf = [
        send(pg.at[1, 0], pg.at[1, e], s_pf.at[e], r_pf.at[e], zdev(4 * FAR[e]))
        for e in range(7, 0, -1)
    ][::-1]
    own_wb.wait()
    c_pn = []
    c_wy = []
    for g, (e, n) in enumerate(GROUPS):
        for c in c_pf[max(e, 1) - 1 : e + n - 1]:
            c.wait_recv()
        c_pn += [
            send(pg.at[1, e : e + n], pg.at[m, e : e + n], s_pn.at[m, g], r_pn.at[m, g], zdev(o))
            for m, o in near
        ]
        for c in c_wb[max(e, 1) - 1 : e + n - 1]:
            c.wait_recv()
        c_wy += [
            send(wg.at[0, e : e + n], wg.at[d, e : e + n], s_wy.at[d, g], r_wy.at[d, g], ydev(d))
            for d in range(1, NY)
        ]
    for c in c_pn:
        c.wait_recv()
    for c in c_wy:
        c.wait_recv()

    line = base // 128
    bias = jnp.concatenate([bias_ref[pl.ds(line + a, 1), :] for a in range(2)], axis=1)
    bias = jnp.broadcast_to(bias, (16, 256))
    bias = pltpu.roll(bias, shift, 1)[:, :128]
    logits = jnp.where(tile_lane < TR, bias, 0.0)
    for k in range(8):
        for m in range(4):
            rows = jnp.concatenate([wg[d, k, m] for d in range(NY)], axis=0)
            logits = logits + lax.dot_general(
                pg[m, k][:, :64], rows, (((1,), (0,)), ((), ())),
                preferred_element_type=jnp.float32,
            )
    rates = jnp.maximum(logits, 0.0) + jnp.log1p(jnp.exp(-jnp.abs(logits))) + rate_floor
    c_cnt.wait()
    observed = pltpu.roll(cnt_ref[...].astype(jnp.float32), shift, 1)[:, :128]
    observed = jnp.where(tile_lane < TR, observed, 0.0)
    part = [
        jnp.sum(rates, axis=0, keepdims=True),
        jnp.sum(observed, axis=0, keepdims=True),
        jnp.sum(observed * jnp.log(rates), axis=0, keepdims=True),
        jnp.zeros((5, 128), jnp.float32),
    ]
    ty[0, 0] = jnp.concatenate(part, axis=0)
    c_ty = [
        send(ty.at[0, 0], ty.at[a, b], s_ty.at[a, b], r_ty.at[a, b], both_dev(a, b))
        for a, b in group
    ]
    sig = 1.0 / (1.0 + jnp.exp(-logits))
    obs_rate = observed / rates
    for c in c_ty:
        c.wait_recv()
    tot = jnp.zeros((8, 128), jnp.float32)
    for a in range(NY):
        for b in range(NS):
            tot = tot + ty[(y + NY - a) % NY, (s + NS - b) % NS]
    pred = tot[0:1, :]
    obs = tot[1:2, :]
    log_pred = jnp.log(pred)
    lane = lax.broadcasted_iota(jnp.int32, (1, 128), 1)
    terms = total_weight * (pred - obs * log_pred) + obs * log_pred - tot[2:3, :]
    loss = jnp.sum(jnp.where(lane < TR, terms, 0.0), axis=1, keepdims=True)
    ratio = obs / pred
    grad_rates = total_weight * (1.0 - ratio) + ratio - obs_rate
    grad = grad_rates * sig
    hi = loss.astype(jnp.bfloat16).astype(jnp.float32)
    mid = (loss - hi).astype(jnp.bfloat16).astype(jnp.float32)
    lo = loss - hi - mid
    lanes = lax.broadcasted_iota(jnp.int32, (16, 128), 1)
    grad = jnp.where(
        lanes < TR, grad, jnp.where(lanes == TR, hi, jnp.where(lanes == TR + 1, mid, lo))
    )
    gg[0, 1, 0] = grad.astype(jnp.bfloat16)
    c_gf = [
        send(gg.at[0, 1, 0], gg.at[0, 1, e], s_gf.at[e], r_gf.at[e], zdev(-4 * FAR[e]))
        for e in range(7, 0, -1)
    ][::-1]
    c_gn = []
    c_gy = []

    def over_y(m, g):
        e, n = GROUPS[g]
        return [
            send(
                gg.at[0, m, e : e + n], gg.at[d, m, e : e + n], s_gy.at[d, m, g],
                r_gy.at[d, m, g], ydev(d),
            )
            for d in range(1, NY)
        ]

    for g in range(5):
        if g < 4:
            e, n = GROUPS[g]
            for c in c_gf[max(e, 1) - 1 : e + n - 1]:
                c.wait_recv()
            c_gn.append(
                [
                    send(
                        gg.at[0, 1, e : e + n], gg.at[0, m, e : e + n], s_gn.at[m, g],
                        r_gn.at[m, g], zdev(-o),
                    )
                    for m, o in near
                ]
            )
            c_gy += over_y(1, g)
        if g > 0:
            for c, (m, o) in zip(c_gn[g - 1], near):
                c.wait_recv()
                c_gy += over_y(m, g - 1)
    c_gn = [c for some in c_gn for c in some]

    by_z = jnp.zeros((1, 128), jnp.float32)
    for k in range(8):
        for m in range(4):
            row = gg[0, m, k][0:1, :].astype(jnp.float32)
            val = jnp.sum(
                jnp.where((lane >= TR) & (lane < TR + 3), row, 0.0), axis=1, keepdims=True
            )
            by_z = jnp.where(lane == (z + m - 1 + 4 * FAR[k] + NZ) % NZ, val, by_z)
    loss_ref[0, 0] = jnp.sum(by_z) * (1.0 / (512 * 3840))


    wl = jnp.concatenate([w_ref[FAR[k], m] for k in range(8) for m in range(4)], axis=1)

    def grad_block(d):
        gl = jnp.concatenate([gg[d, m, k] for k in range(8) for m in range(4)], axis=1)
        block = lax.dot_general(wl, gl, nt, preferred_element_type=jnp.float32)
        top, low = halves(block)
        for j in range(4):
            rows = lax.dot_general(top, spread[j], nn, preferred_element_type=jnp.float32)
            rows = rows + lax.dot_general(low, spread[j], nn, preferred_element_type=jnp.float32)
            oo[pl.ds((y + NY - d) % NY * 4 + j, 16, stride=16), :] = rows

    grad_block(0)
    for c in c_gy:
        c.wait_recv()
    for d in range(1, NY):
        grad_block(d)

    gated = oo[...] * query
    gg_out[...] = gated.astype(jnp.bfloat16).reshape(NS, 2, 16, 128)
    c_gx = [
        send(gg_out.at[(s + d) % NS], gx.at[d], s_gx.at[d], r_gx.at[d], sdev(d))
        for d in range(1, NS)
    ]
    gx[0] = gg_out[s]

    def give(p):
        for a in range(16):
            out_ref[p, :, 128 * a : 128 * a + 128] = mx[pl.ds(a, 16, stride=16), :]

    mx[...] = oo[...] * mx[...]
    give(0)
    for c in c_cv:
        c.wait_send()
    for c in c_gx:
        c.wait_recv()
    place(gx)

    def backward(c, carry):
        for d in range(16):
            sh[c, :, 128 * d : 128 * d + 128] = xp[c, 16 + d : 144 + d, :].astype(jnp.bfloat16)
        for p in range(4):
            taps = jnp.concatenate(
                [
                    jnp.concatenate([tt[c, 32 * p + 16 * h + e] for e in range(16)], axis=1)
                    for h in range(2)
                ],
                axis=0,
            )
            rows = 128 - 32 * p
            part = lax.dot_general(
                sh[c, 32 * p : 128, :], taps, nt, preferred_element_type=jnp.float32
            )
            first = part[:, :128].reshape(8 - 2 * p, 16, 128)
            second = part[16:, 128:].reshape(7 - 2 * p, 16, 128)
            if p == 0:
                yy[c] = first
            else:
                yy[c, 0 : 8 - 2 * p] = yy[c, 0 : 8 - 2 * p] + first
            yy[c, 0 : 7 - 2 * p] = yy[c, 0 : 7 - 2 * p] + second
        return carry

    for c in range(2):
        backward(c, 0)
    yb[...] = yy[...].astype(jnp.bfloat16)
    c_gr = [
        send(yb.at[:, (s + d) % NS], gr.at[d], s_gr.at[d], r_gr.at[d], sdev(d))
        for d in range(1, NS)
    ]
    gr[0] = yb[:, s]
    for c in c_gr:
        c.wait_recv()
    grad_kv = collect(gr) + skip * (oo[...] * query)
    mx[...] = grad_kv * x_ref[2]
    give(1)
    mx[...] = grad_kv * x_ref[1]
    give(2)

    for c in c_hx + c_kv + c_wa + c_py + c_wb + c_pf + c_pn + c_wy + c_ty:
        c.wait_send()
    for c in c_gf + c_gn + c_gy + c_gx + c_gr:
        c.wait_send()


def per_device(projections, filter_taps, skip_gain, head_weight, head_bias, counts):
    sem = pltpu.SemaphoreType.DMA
    b16 = jnp.bfloat16
    f32 = jnp.float32
    out, loss = pl.pallas_call(
        step_kernel,
        out_shape=(
            jax.ShapeDtypeStruct((3, 16, 2048), f32),
            jax.ShapeDtypeStruct((1, 1), f32),
        ),
        in_specs=[
            pl.BlockSpec(memory_space=space)
            for space in (pltpu.VMEM, pltpu.VMEM, pltpu.SMEM, pltpu.VMEM, pl.ANY, pltpu.VMEM)
        ],
        out_specs=(
            pl.BlockSpec(memory_space=pltpu.VMEM),
            pl.BlockSpec(memory_space=pltpu.SMEM),
        ),
        scratch_shapes=[
            pltpu.VMEM((3, 256, 128), f32),
            pltpu.VMEM((256, 128), f32),
            pltpu.VMEM((8, 2, 16, 128), b16),
            pltpu.VMEM((8, 4, 16, 128), b16),
            pltpu.VMEM((16, 256), jnp.int32),
            pltpu.VMEM((256, 128), f32),
            pltpu.VMEM((8, 2, 16, 128), b16),
            pltpu.VMEM((7, 2, 16, 128), b16),
            pltpu.VMEM((8, 2, 16, 128), b16),
            pltpu.VMEM((2, 160, 128), f32),
            pltpu.VMEM((2, 128, 128), f32),
            pltpu.VMEM((2, 1032, 128), f32),
            pltpu.VMEM((2, 1024, 256), b16),
            pltpu.VMEM((8, 256, 256), b16),
            pltpu.VMEM((2, 128, 2048), b16),
            pltpu.VMEM((2, 128, 128, 128), b16),
            pltpu.VMEM((2, 8, 16, 128), f32),
            pltpu.VMEM((2, 8, 16, 128), b16),
            pltpu.VMEM((8, 2, 16, 128), b16),
            pltpu.VMEM((256, 128), f32),
            pltpu.VMEM((8, 2, 16, 128), b16),
            pltpu.VMEM((8, 2, 16, 128), b16),
            pltpu.VMEM((8, 2, 16, 128), b16),
            pltpu.VMEM((4, 16, 128), b16),
            pltpu.VMEM((4, 8, 16, 128), b16),
            pltpu.VMEM((4, 8, 4, 16, 128), b16),
            pltpu.VMEM((3, 16, 128), b16),
            pltpu.VMEM((4, 8, 16, 128), b16),
            pltpu.VMEM((4, 8, 8, 128), f32),
            pltpu.VMEM((4, 4, 8, 16, 128), b16),
            pltpu.SemaphoreType.REGULAR((3, 2)),
            sem((3,)),
            sem((8,)), sem((8,)), sem((8,)), sem((8,)), sem((8,)), sem((8,)),
            sem((8,)), sem((8,)), sem((8,)), sem((8,)),
            sem((4,)), sem((4,)), sem((8,)), sem((8,)), sem((4, 4)), sem((4, 4)),
            sem((4,)), sem((4,)), sem((8,)), sem((8,)), sem((4, 4)), sem((4, 4)),
            sem((4, 8)), sem((4, 8)), sem((8,)), sem((8,)),
            sem((4, 4)), sem((4, 4)), sem((4, 4, 4)), sem((4, 4, 4)),
        ],
        compiler_params=pltpu.CompilerParams(collective_id=0, has_side_effects=True),
    )(projections, filter_taps, skip_gain, head_weight, counts, head_bias.reshape(-1, 128))
    return loss.reshape(()), out


def solution(mesh):
    placed = (
        P(None, "chan", "seq"),
        P("chan", "seq"),
        P("chan"),
        P("chan", None),
        P(),
        P("seq", None),
    )
    return jax.shard_map(
        per_device,
        mesh=mesh,
        in_specs=placed,
        out_specs=(P(), P(None, "chan", "seq")),
        check_vma=False,
    )
```
